256 devices in a mesh: expert: 128 (over x, z, y), dp: 2 (over core).
Axes of the slice: x: 4, y: 4, z: 8, core: 2. Of those that a mesh axis runs over, the one named last changes fastest.
Arguments:
- tokens: bfloat16 [16384, 4096], P(('expert', 'dp')), may hold values from -6 to 6
- routes: int32 [16384, 8], P(('expert', 'dp')), may hold values from 0 to 127, all different within a row; in each aligned block of 64 rows (0 to 63, 64 to 127, ...) at most 8 rows name the same one
- gate_probs: float32 [16384, 8], P(('expert', 'dp')), may hold values from 0.05 to 0.35
- gate_w: bfloat16 [128, 4096, 768], P('expert', None, 'dp'), may hold values from -0.09375 to 0.09375
- up_w: bfloat16 [128, 4096, 768], P('expert', None, 'dp'), may hold values from -0.09375 to 0.09375
- down_w: bfloat16 [128, 768, 4096], P('expert', 'dp'), may hold values from -0.21875 to 0.21875
Outputs:
- mixed_out: bfloat16 [16384, 4096], P(('expert', 'dp'))
The draws below stay inside these ranges and needn't reach their ends.
Inputs may be any that keep to these rules, and one draw needn't show every extreme that they name: `routes`: each token names 8 different experts. Among the 64 tokens of one device (aligned blocks of rows), no expert is named by more than 8 tokens; in some block an expert is named by exactly 8 tokens.
All inputs are finite; a program needn't handle non-finite values.
Results may differ from the reference program's by a relative error of at most 0.0057.
Values may be sent and summed in bfloat16 or wider, within the bound.
No kernel may reach another device: no remote copies, remote signals or barrier semaphores. Data moves between devices by JAX's collectives and lax.ppermute only.
A program may use at most 192 MiB of HBM per device.

```python
import math
import jax
import jax.numpy as jnp
import numpy as np
from jax import lax

D = 4096
HID = 768
TOP = 8
TOK_DEV = 64
EXPERTS = 128
CAP = 8
TOKENS = 16384


def level_of(key, shape, split, low, largest):
    def one(dim, shards_of):
        heights = jax.random.uniform(jax.random.fold_in(jax.random.fold_in(key, 6), dim), (shards_of,), jnp.float32, low / len(split), largest / len(split))
        return jnp.repeat(jnp.exp(heights), shape[dim] // shards_of).reshape((-1,) + (1,) * (len(shape) - dim - 1))

    loudness = one(*split[0])
    for cut in split[1:]:
        loudness = loudness * one(*cut)
    return loudness


def deal_out(key, own, number, rows, count, top, limit, lean):
    ranking = jax.random.permutation(key, count)
    heavy_load, common = shares(count, rows * top, limit, lean, True), shares(count, rows * top, limit, lean, False)
    places = jnp.arange(count)

    def named(tallies, rotation):
        used = int((tallies > 0).sum())
        fixed = max(1, used // 4)
        shifted = fixed + (places - fixed + rotation * (used - fixed)) % max(1, count - fixed)
        return jnp.zeros((count,), jnp.int32).at[ranking[jnp.where(places < fixed, places, shifted)]].set(jnp.asarray(tallies, jnp.int32))

    tallies = jnp.where(number % 4 == 0, named(heavy_load, number // 4), named(common, number - number // 4 - 1))
    mixed = jax.random.permutation(jax.random.fold_in(own, 3), count)
    donor, taker = mixed[0:count // 2 * 2:2], mixed[1:count // 2 * 2:2]
    margin = jnp.minimum(tallies[donor] - 1, limit - tallies[taker]) // 2
    margin = jnp.where((donor == ranking[0]) | (taker == ranking[0]) | (tallies[taker] == 0), 0, jnp.maximum(margin, 0))
    shifted = jax.random.randint(jax.random.fold_in(own, 4), (count // 2,), 0, 1 << 20) % (margin + 1)
    tallies = tallies.at[donor].add(-shifted).at[taker].add(shifted)
    items = jnp.searchsorted(jnp.cumsum(tallies), jnp.arange(rows * top), side="right").astype(jnp.int32)
    table = items.reshape(top, rows).T
    table = table[jax.random.permutation(jax.random.fold_in(own, 1), rows)]
    rotation = jax.random.randint(jax.random.fold_in(own, 2), (rows, 1), 0, top)
    return jnp.take_along_axis(table, (jnp.arange(top)[None, :] + rotation) % top, axis=1)


def shares(number_of, total, bound, lean, full):
    loads = [(1 << 20) // math.isqrt(standing ** lean) + 1 for standing in range(1, number_of + 1)]
    largest = bound if full else min(bound, max(-(-total // number_of), total * loads[0] // sum(loads)))
    least = 1 if total - largest >= number_of - 1 else 0
    given, spare = [largest] + [least] * (number_of - 1), total - largest - least * (number_of - 1)
    while spare > 0:
        candidates = [i for i in range(1, number_of) if given[i] < largest] or [i for i in range(1, number_of) if given[i] < bound]
        pool, remaining = sum([loads[i] for i in candidates]), spare
        for i in candidates:
            more = min(bound - given[i], max(1, remaining * loads[i] // pool), spare)
            given[i] = given[i] + more
            spare = spare - more
    return np.array(given)


def normal_values(key, dims, width, most, pieces=(), kind=jnp.bfloat16):
    entries = width * jax.random.normal(key, dims, jnp.float32)
    if pieces:
        entries = entries * level_of(key, dims, pieces, -0.22, 0.18)
    return jnp.clip(entries, -most, most).astype(kind)


def setup_inputs(seed: int = 0) -> dict:
    seeds = jax.random.split(jax.random.key(seed), 7)
    tokens = normal_values(seeds[0], (TOKENS, D), 1.0, 6.0, ((0, 256),))
    routes_keys = jax.random.split(jax.random.fold_in(seeds[1], 1), TOKENS // TOK_DEV)
    routes_turns = jax.random.permutation(jax.random.fold_in(seeds[1], 3), TOKENS // TOK_DEV)
    routes = jax.vmap(lambda own, number: deal_out(jax.random.fold_in(seeds[1], 2), own, number, TOK_DEV, EXPERTS, TOP, CAP, 2))(routes_keys, routes_turns).reshape((TOKENS, TOP))
    gate_probs = jnp.clip(0.05 + 0.29999999 * jax.random.uniform(seeds[2], (TOKENS, TOP), jnp.float32) ** level_of(seeds[2], (TOKENS, TOP), ((0, 256),), -0.2, 0.2), 0.05, 0.35)
    gate_w = normal_values(seeds[3], (EXPERTS, D, HID), D ** -0.5, 0.09375, ((0, 128), (2, 2)))
    up_w = normal_values(seeds[4], (EXPERTS, D, HID), D ** -0.5, 0.09375, ((0, 128), (2, 2)))
    down_w = normal_values(seeds[5], (EXPERTS, HID, D), HID ** -0.5, 0.21875, ((0, 128), (1, 2)))
    return dict(tokens=tokens, routes=routes, gate_probs=gate_probs, gate_w=gate_w, up_w=up_w, down_w=down_w)


def reference(tokens, routes, gate_probs, gate_w, up_w, down_w):
    device_count = TOKENS // TOK_DEV
    local_routes = routes.reshape(device_count, TOK_DEV, TOP)
    expert_ids = jnp.arange(EXPERTS, dtype=jnp.int32)
    named_hits = jnp.sum((local_routes[..., None] == expert_ids).astype(jnp.int32), axis=2)
    before = jnp.cumsum(named_hits, axis=1) - named_hits
    slot_index = jnp.take_along_axis(before, local_routes, axis=2)
    sources = jnp.arange(device_count, dtype=jnp.int32)[:, None, None]
    buffer_row = (sources * CAP + slot_index).reshape(TOKENS, TOP).astype(jnp.int32)
    token_ids = jnp.broadcast_to(jnp.arange(TOKENS, dtype=jnp.int32)[:, None], (TOKENS, TOP))
    source_table = jnp.full((EXPERTS, device_count * CAP), TOKENS, jnp.int32).at[routes, buffer_row].set(token_ids)
    weight_table = jnp.zeros((EXPERTS, device_count * CAP), jnp.float32).at[routes, buffer_row].set(gate_probs.astype(jnp.float32))
    padded = jnp.concatenate([tokens, jnp.zeros((1, D), tokens.dtype)], axis=0)

    def expert_pass(running, inputs):
        row_ids, row_weights, gate_part, up_part, down_part = inputs
        gathered = padded[row_ids]
        gate_act = jnp.dot(gathered, gate_part, preferred_element_type=jnp.float32)
        up_act = jnp.dot(gathered, up_part, preferred_element_type=jnp.float32)
        hidden = (jax.nn.silu(gate_act) * up_act).astype(jnp.bfloat16)
        expert_out = jnp.dot(hidden, down_part, preferred_element_type=jnp.float32).astype(jnp.bfloat16)
        running = running.at[row_ids].add(row_weights[:, None] * expert_out.astype(jnp.float32), mode="drop")
        return running, None

    start = jnp.zeros((TOKENS, D), jnp.float32)
    total, _ = lax.scan(expert_pass, start, (source_table, weight_table, gate_w, up_w, down_w))
    return total.astype(jnp.bfloat16)
```

```python
import jax
import jax.numpy as jnp
from jax import lax
from jax.experimental import pallas as pl
from jax.experimental.pallas import tpu as pltpu
from jax.sharding import Mesh
from jax.sharding import PartitionSpec as P

PLANE = ("x", "y")


def slot_table(routes, gate_probs, experts, capacity):
    tok_count, top_count = routes.shape
    flat = routes.T.reshape(-1)
    token = jnp.arange(tok_count * top_count, dtype=jnp.int32) % tok_count
    earlier = (flat[:, None] == flat[None, :]) & (token[None, :] < token[:, None])
    slot = jnp.sum(earlier.astype(jnp.int32), axis=1)
    target = flat * capacity + slot
    slots = jnp.arange(experts * capacity, dtype=jnp.int32)
    here = target[None, :] == slots[:, None]
    held = jnp.sum(jnp.where(here, (token + 1).astype(jnp.float32)[None, :], 0.0), axis=1)
    prob = jnp.sum(jnp.where(here, gate_probs.T.reshape(-1)[None, :], 0.0), axis=1)
    return held, prob


def mix_kernel(weight_ref, rows_ref, out_ref):
    sums = jnp.dot(weight_ref[...], rows_ref[...], preferred_element_type=jnp.float32)
    half = out_ref.shape[0]
    out_ref[...] = (sums[:half] + sums[half:]).astype(out_ref.dtype)


def mix(weight, rows, width=512):
    high = weight.astype(jnp.bfloat16)
    low = (weight - high.astype(jnp.float32)).astype(jnp.bfloat16)
    parts = jnp.concatenate([high, low], axis=0)
    return pl.pallas_call(
        mix_kernel,
        grid=(rows.shape[1] // width,),
        in_specs=[
            pl.BlockSpec(parts.shape, lambda i: (0, 0), pipeline_mode=pl.Buffered(1)),
            pl.BlockSpec((rows.shape[0], width), lambda i: (0, i)),
        ],
        out_specs=pl.BlockSpec((weight.shape[0], width), lambda i: (0, i)),
        out_shape=jax.ShapeDtypeStruct((weight.shape[0], rows.shape[1]), jnp.bfloat16),
        name="mix",
    )(parts, rows)


def body(tokens, routes, gate_probs, gate_w, up_w, down_w):
    x_size, z_size, y_size = lax.axis_size("x"), lax.axis_size("z"), lax.axis_size("y")
    experts = x_size * z_size * y_size
    plane = x_size * y_size
    tok_count, model_width = tokens.shape
    capacity = 2 * tok_count * routes.shape[1] // experts
    my_z = lax.axis_index("z")

    all_tokens = lax.all_gather(tokens, "z", axis=0, tiled=True)

    swap = [(0, 1), (1, 0)]
    w_gate = jnp.concatenate([gate_w[0], lax.ppermute(gate_w[0], "dp", swap)], axis=1)
    w_up = jnp.concatenate([up_w[0], lax.ppermute(up_w[0], "dp", swap)], axis=1)
    w_down = jnp.concatenate([down_w[0], lax.ppermute(down_w[0], "dp", swap)], axis=0)

    held, prob = slot_table(routes, gate_probs, experts, capacity)
    table = jnp.stack([held, prob]).reshape(2, x_size, z_size, y_size * capacity)
    table = table.transpose(2, 0, 1, 3)
    parts, sources = [], []
    for d in range(z_size):
        mine = lax.dynamic_index_in_dim(table, (my_z + d) % z_size, 0, keepdims=False)
        if d:
            mine = lax.ppermute(mine, "z", [(i, (i + d) % z_size) for i in range(z_size)])
        parts.append(mine.reshape(2, plane, capacity))
        sources.append((my_z - d) % z_size)
    parts = jnp.stack(parts, axis=2)
    source = jnp.stack(sources)[None, :, None]
    rows_here = plane * z_size * capacity
    held_row = parts[0].astype(jnp.int32)
    token_id = jnp.where(held_row > 0, source * tok_count + held_row - 1, -1).reshape(rows_here)
    weight = parts[1].reshape(rows_here)

    ring_ids = jnp.arange(z_size * tok_count, dtype=jnp.int32)
    placer = (token_id[:, None] == ring_ids[None, :]).astype(jnp.bfloat16)
    mixer = jnp.where(ring_ids[:, None] == token_id[None, :], weight[None, :], 0.0)

    outgoing = jnp.dot(placer, all_tokens, preferred_element_type=jnp.float32).astype(jnp.bfloat16)
    outgoing = outgoing.reshape(plane, rows_here // plane, model_width)
    rows = lax.all_to_all(outgoing, PLANE, split_axis=0, concat_axis=0, tiled=True)
    rows = rows.reshape(rows_here, model_width)
    gate_act = jnp.dot(rows, w_gate, preferred_element_type=jnp.float32)
    up_act = jnp.dot(rows, w_up, preferred_element_type=jnp.float32)
    hidden = (jax.nn.silu(gate_act) * up_act).astype(jnp.bfloat16)
    answers = jnp.dot(hidden, w_down, preferred_element_type=jnp.float32).astype(jnp.bfloat16)
    answers = answers.reshape(plane, rows_here // plane, model_width)
    returned = lax.all_to_all(answers, PLANE, split_axis=0, concat_axis=0, tiled=True)
    partial = mix(mixer, returned.reshape(rows_here, model_width))
    return lax.psum_scatter(partial, "z", scatter_dimension=0, tiled=True)


def solution(mesh):
    experts, dp = mesh.shape["expert"], mesh.shape["dp"]
    x_size = y_size = 4
    z_size = experts // (x_size * y_size)
    grid = Mesh(mesh.devices.reshape(x_size, z_size, y_size, dp), ("x", "z", "y", "dp"))
    every, owner = ("x", "z", "y", "dp"), ("x", "z", "y")
    return jax.shard_map(
        body,
        mesh=grid,
        in_specs=(
            P(every, None),
            P(every, None),
            P(every, None),
            P(owner, None, "dp"),
            P(owner, None, "dp"),
            P(owner, "dp", None),
        ),
        out_specs=P(every, None),
        check_vma=False,
    )
```

```python
import functools

import jax
import jax.numpy as jnp
from jax import lax
from jax.experimental import pallas as pl
from jax.experimental.pallas import tpu as pltpu
from jax.sharding import Mesh
from jax.sharding import PartitionSpec as P

WIDTH = 256
DIRECT = 768


def slot_table(routes, gate_probs, sizes, capacity):
    x_size, z_size, y_size = sizes
    tok_count, top_count = routes.shape
    flat = routes.T.reshape(-1)
    token = jnp.arange(tok_count * top_count, dtype=jnp.int32) % tok_count
    earlier = (flat[:, None] == flat[None, :]) & (token[None, :] < token[:, None])
    slot = jnp.sum(earlier.astype(jnp.int32), axis=1)
    ex, ez, ey = flat // (z_size * y_size), flat // y_size % z_size, flat % y_size
    target = ((ez * x_size + ex) * y_size + ey) * capacity + slot
    slots = jnp.arange(x_size * z_size * y_size * capacity, dtype=jnp.int32)
    here = target[None, :] == slots[:, None]
    held = jnp.sum(jnp.where(here, (token + 1).astype(jnp.float32)[None, :], 0.0), axis=1)
    prob = jnp.sum(jnp.where(here, gate_probs.T.reshape(-1)[None, :], 0.0), axis=1)
    return jnp.stack([held.reshape(z_size, -1), prob.reshape(z_size, -1)], axis=1)


def hits(table_ref, i, tok_count):
    row_token = table_ref[i, 0:1, :].astype(jnp.int32) - 1
    lanes = row_token.shape[1]
    return lax.broadcasted_iota(jnp.int32, (tok_count, lanes), 0) == row_token


def pack_kernel(order_ref, table_ref, tok_ref, out_ref):
    groups = table_ref.shape[0]
    sources, tok_count, width = tok_ref.shape
    plane, _, capacity, _ = out_ref.shape
    for i in range(groups):
        src = order_ref[i]
        block = tok_ref[src] if sources > 1 else tok_ref[0]
        place = jnp.where(hits(table_ref, i, tok_count), 1.0, 0.0).astype(jnp.bfloat16)
        rows = lax.dot_general(
            place, block, (((0,), (0,)), ((), ())), preferred_element_type=jnp.float32
        )
        out_ref[:, src] = rows.astype(jnp.bfloat16).reshape(plane, capacity, width)


def pack(order, table, tok, plane, capacity):
    groups = table.shape[0]
    sources, tok_count, width = tok.shape
    return pl.pallas_call(
        pack_kernel,
        grid_spec=pltpu.PrefetchScalarGridSpec(
            num_scalar_prefetch=1,
            grid=(width // WIDTH,),
            in_specs=[
                pl.BlockSpec(table.shape, lambda i, order: (0, 0, 0)),
                pl.BlockSpec((sources, tok_count, WIDTH), lambda i, order: (0, 0, i)),
            ],
            out_specs=pl.BlockSpec((plane, groups, capacity, WIDTH), lambda i, order: (0, 0, 0, i)),
        ),
        out_shape=jax.ShapeDtypeStruct((plane, groups, capacity, width), tok.dtype),
        name="pack",
    )(order, table, tok)


def mix_kernel(order_ref, table_ref, rows_ref, out_ref):
    groups = table_ref.shape[0]
    outs, tok_count, width = out_ref.shape
    plane, _, capacity, _ = rows_ref.shape
    total = None
    for i in range(groups):
        src = order_ref[i]
        prob = jnp.where(hits(table_ref, i, tok_count), table_ref[i, 1:2, :], 0.0)
        high = prob.astype(jnp.bfloat16)
        low = (prob - high.astype(jnp.float32)).astype(jnp.bfloat16)
        rows = rows_ref[:, src].reshape(plane * capacity, width)
        both = jnp.concatenate([high, low], axis=0)
        sums = jnp.dot(both, rows, preferred_element_type=jnp.float32)
        sums = sums[:tok_count] + sums[tok_count:]
        if outs > 1:
            out_ref[src] = sums.astype(out_ref.dtype)
        else:
            total = sums if total is None else total + sums
    if outs == 1:
        out_ref[0] = total.astype(out_ref.dtype)


def mix(order, table, rows, tok_count, outs):
    plane, groups, capacity, width = rows.shape
    return pl.pallas_call(
        mix_kernel,
        grid_spec=pltpu.PrefetchScalarGridSpec(
            num_scalar_prefetch=1,
            grid=(width // WIDTH,),
            in_specs=[
                pl.BlockSpec(table.shape, lambda i, order: (0, 0, 0)),
                pl.BlockSpec((plane, groups, capacity, WIDTH), lambda i, order: (0, 0, 0, i)),
            ],
            out_specs=pl.BlockSpec((outs, tok_count, WIDTH), lambda i, order: (0, 0, i)),
        ),
        out_shape=jax.ShapeDtypeStruct((outs, tok_count, width), jnp.bfloat16),
        name="mix",
    )(order, table, rows)


def dot(a, b):
    return jnp.dot(a, b, preferred_element_type=jnp.float32)


def body(tokens, routes, gate_probs, gate_w, up_w, down_w):
    sizes = tuple(lax.axis_size(a) for a in ("x", "z", "y"))
    x_size, z_size, y_size = sizes
    plane = x_size * y_size
    tok_count, model_width = tokens.shape
    capacity = 2 * tok_count * routes.shape[1] // (plane * z_size)
    rows_here = plane * z_size * capacity
    my_z = lax.axis_index("z")
    exchange = functools.partial(lax.all_to_all, split_axis=0, concat_axis=0, tiled=True)

    def in_plane(rows):
        width = rows.shape[-1]
        rows = exchange(rows.reshape(plane, z_size * capacity, width), ("x", "y"))
        return rows.reshape(plane, z_size, capacity, width)

    def direct(rows):
        width = rows.shape[-1]
        rows = exchange(rows.reshape(plane * z_size, capacity, width), ("x", "y", "z"))
        return rows.reshape(plane, z_size, capacity, width)

    first, rest = tokens[:, :DIRECT], tokens[:, DIRECT:]
    all_rest = lax.all_gather(rest, "z", axis=0, tiled=False)

    table = slot_table(routes, gate_probs, sizes, capacity)
    plain = jnp.arange(z_size, dtype=jnp.int32)
    rows_first = direct(pack(plain, table, first[None], plane, capacity))

    swap = [(0, 1), (1, 0)]

    def whole(w, axis):
        return jnp.concatenate([w, lax.ppermute(w, "dp", swap)], axis=axis)

    w_gate, w_up, w_down = whole(gate_w[0], 1), whole(up_w[0], 1), whole(down_w[0], 0)

    parts = []
    for d in range(z_size):
        mine = lax.dynamic_index_in_dim(table, (my_z + d) % z_size, 0, keepdims=False)
        if d:
            mine = lax.ppermute(mine, "z", [(i, (i + d) % z_size) for i in range(z_size)])
        parts.append(mine)
    ring_table = jnp.stack(parts)
    ring_order = (my_z - plain) % z_size

    flat_first = rows_first.reshape(rows_here, DIRECT)
    gate_first, up_first = dot(flat_first, w_gate[:DIRECT]), dot(flat_first, w_up[:DIRECT])
    all_rest, gate_first, up_first, w_gate, w_up, w_down, ring_table, ring_order = (
        lax.optimization_barrier(
            (all_rest, gate_first, up_first, w_gate, w_up, w_down, ring_table, ring_order)
        )
    )
    rows_rest = in_plane(pack(ring_order, ring_table, all_rest, plane, capacity))
    flat_rest = rows_rest.reshape(rows_here, model_width - DIRECT)
    gate_act = gate_first + dot(flat_rest, w_gate[DIRECT:])
    up_act = up_first + dot(flat_rest, w_up[DIRECT:])
    hidden = (jax.nn.silu(gate_act) * up_act).astype(jnp.bfloat16)

    answers = dot(hidden, w_down[:, DIRECT:]).astype(jnp.bfloat16)
    back_rest = in_plane(answers.reshape(plane, z_size, capacity, model_width - DIRECT))
    partial = mix(ring_order, ring_table, back_rest, tok_count, z_size)
    partial, hidden = lax.optimization_barrier((partial, hidden))
    out_rest = lax.psum_scatter(partial, "z", scatter_dimension=0, tiled=True)[0]

    answers = dot(hidden, w_down[:, :DIRECT]).astype(jnp.bfloat16)
    back_first = direct(answers.reshape(plane, z_size, capacity, DIRECT))
    out_first = mix(plain, table, back_first, tok_count, 1)[0]
    return jnp.concatenate([out_first, out_rest], axis=1)


def solution(mesh):
    experts, dp = mesh.shape["expert"], mesh.shape["dp"]
    x_size = y_size = 4
    z_size = experts // (x_size * y_size)
    grid = Mesh(mesh.devices.reshape(x_size, z_size, y_size, dp), ("x", "z", "y", "dp"))
    every, owner = ("x", "z", "y", "dp"), ("x", "z", "y")
    return jax.shard_map(
        body,
        mesh=grid,
        in_specs=(
            P(every, None),
            P(every, None),
            P(every, None),
            P(owner, None, "dp"),
            P(owner, None, "dp"),
            P(owner, "dp", None),
        ),
        out_specs=P(every, None),
        check_vma=False,
    )
```

```python
import jax
import jax.numpy as jnp
import numpy as np
from jax import lax
from jax.experimental import pallas as pl
from jax.experimental.pallas import tpu as pltpu
from jax.sharding import Mesh
from jax.sharding import PartitionSpec as P

ARRIVE = (1536, 2560)
LEAVE = (2048, 2048)


def slot_table(routes, gate_probs, sizes, capacity):
    x_size, z_size, y_size = sizes
    tok_count, top_count = routes.shape
    flat = routes.T.reshape(-1)
    token = jnp.arange(tok_count * top_count, dtype=jnp.int32) % tok_count
    earlier = (flat[:, None] == flat[None, :]) & (token[None, :] < token[:, None])
    slot = jnp.sum(earlier.astype(jnp.int32), axis=1)
    ex, ez, ey = flat // (z_size * y_size), flat // y_size % z_size, flat % y_size
    target = ((ez * x_size + ex) * y_size + ey) * capacity + slot
    slots = jnp.arange(x_size * z_size * y_size * capacity, dtype=jnp.int32)
    here = target[None, :] == slots[:, None]
    held = jnp.sum(jnp.where(here, (token + 1).astype(jnp.float32)[None, :], 0.0), axis=1)
    prob = jnp.sum(jnp.where(here, gate_probs.T.reshape(-1)[None, :], 0.0), axis=1)
    return jnp.stack([held.reshape(z_size, -1), prob.reshape(z_size, -1)], axis=1)


def hits(table_ref, i, tok_count):
    row_token = table_ref[i, 0:1, :].astype(jnp.int32) - 1
    lanes = row_token.shape[1]
    return lax.broadcasted_iota(jnp.int32, (tok_count, lanes), 0) == row_token


def pack_kernel(order_ref, table_ref, tok_ref, out_ref):
    plane, _, capacity, width = out_ref.shape
    tok_count = tok_ref.shape[1]
    place = jnp.where(hits(table_ref, 0, tok_count), 1.0, 0.0).astype(jnp.bfloat16)
    rows = lax.dot_general(
        place, tok_ref[0], (((0,), (0,)), ((), ())), preferred_element_type=jnp.float32
    )
    out_ref[:, 0] = rows.astype(jnp.bfloat16).reshape(plane, capacity, width)


def pack(order, table, tok, plane, capacity):
    sources, tok_count, width = tok.shape
    return pl.pallas_call(
        pack_kernel,
        grid_spec=pltpu.PrefetchScalarGridSpec(
            num_scalar_prefetch=1,
            grid=(sources,),
            in_specs=[
                pl.BlockSpec((1,) + table.shape[1:], lambda i, order: (i, 0, 0)),
                pl.BlockSpec((1, tok_count, width), lambda i, order: (order[i], 0, 0)),
            ],
            out_specs=pl.BlockSpec(
                (plane, 1, capacity, width), lambda i, order: (0, order[i], 0, 0)
            ),
        ),
        out_shape=jax.ShapeDtypeStruct((plane, sources, capacity, width), tok.dtype),
        name="pack",
    )(order, table, tok)


def mix_kernel(order_ref, table_ref, rows_ref, out_ref):
    plane, _, capacity, width = rows_ref.shape
    tok_count = out_ref.shape[1]
    prob = jnp.where(hits(table_ref, 0, tok_count), table_ref[0, 1:2, :], 0.0)
    high = prob.astype(jnp.bfloat16)
    low = (prob - high.astype(jnp.float32)).astype(jnp.bfloat16)
    rows = rows_ref[:, 0].reshape(plane * capacity, width)
    sums = jnp.dot(jnp.concatenate([high, low], axis=0), rows, preferred_element_type=jnp.float32)
    out_ref[0] = (sums[:tok_count] + sums[tok_count:]).astype(out_ref.dtype)


def mix(order, table, rows, tok_count):
    plane, sources, capacity, width = rows.shape
    return pl.pallas_call(
        mix_kernel,
        grid_spec=pltpu.PrefetchScalarGridSpec(
            num_scalar_prefetch=1,
            grid=(sources,),
            in_specs=[
                pl.BlockSpec((1,) + table.shape[1:], lambda i, order: (i, 0, 0)),
                pl.BlockSpec((plane, 1, capacity, width), lambda i, order: (0, order[i], 0, 0)),
            ],
            out_specs=pl.BlockSpec((1, tok_count, width), lambda i, order: (order[i], 0, 0)),
        ),
        out_shape=jax.ShapeDtypeStruct((sources, tok_count, width), jnp.bfloat16),
        name="mix",
    )(order, table, rows)


def cuts(widths):
    ends = np.cumsum(widths)
    return [slice(int(end) - width, int(end)) for width, end in zip(widths, ends, strict=True)]


def dot(a, b):
    return jnp.dot(a, b, preferred_element_type=jnp.float32)


def body(tokens, routes, gate_probs, gate_w, up_w, down_w):
    sizes = tuple(lax.axis_size(a) for a in ("x", "z", "y"))
    x_size, z_size, y_size = sizes
    plane = x_size * y_size
    tok_count, model_width = tokens.shape
    capacity = 2 * tok_count * routes.shape[1] // (plane * z_size)
    rows_here = plane * z_size * capacity
    my_z = lax.axis_index("z")
    def in_plane(rows):
        width = rows.shape[-1]
        rows = rows.reshape(plane, z_size * capacity, width)
        rows = lax.all_to_all(rows, ("x", "y"), split_axis=0, concat_axis=0, tiled=True)
        return rows.reshape(plane, z_size, capacity, width)

    into, back = cuts(ARRIVE), cuts(LEAVE)
    gathered = [lax.all_gather(tokens[:, part], "z", axis=0, tiled=False) for part in into]

    table = slot_table(routes, gate_probs, sizes, capacity)
    swap = [(0, 1), (1, 0)]

    def whole(w, axis):
        return jnp.concatenate([w, lax.ppermute(w, "dp", swap)], axis=axis)

    w_gate, w_up, w_down = whole(gate_w[0], 1), whole(up_w[0], 1), whole(down_w[0], 0)

    parts = []
    for d in range(z_size):
        mine = lax.dynamic_index_in_dim(table, (my_z + d) % z_size, 0, keepdims=False)
        if d:
            mine = lax.ppermute(mine, "z", [(i, (i + d) % z_size) for i in range(z_size)])
        parts.append(mine)
    ring_table = jnp.stack(parts)
    ring_order = (my_z - jnp.arange(z_size, dtype=jnp.int32)) % z_size

    ready = (w_gate, w_up, w_down, ring_table, ring_order)
    gate_act = up_act = 0.0
    for part, block in zip(into, gathered, strict=True):
        block, ready, gate_act, up_act = lax.optimization_barrier((block, ready, gate_act, up_act))
        w_gate, w_up, w_down, ring_table, ring_order = ready
        rows = in_plane(pack(ring_order, ring_table, block, plane, capacity))
        rows = rows.reshape(rows_here, -1)
        gate_act += dot(rows, w_gate[part])
        up_act += dot(rows, w_up[part])
    hidden = (jax.nn.silu(gate_act) * up_act).astype(jnp.bfloat16)

    outs = []
    for part in back:
        answers = dot(hidden, w_down[:, part]).astype(jnp.bfloat16)
        rows = in_plane(answers.reshape(plane, z_size, capacity, -1))
        partial = mix(ring_order, ring_table, rows, tok_count)
        partial, hidden = lax.optimization_barrier((partial, hidden))
        outs.append(lax.psum_scatter(partial, "z", scatter_dimension=0, tiled=True)[0])
    return jnp.concatenate(outs, axis=1)


def solution(mesh):
    experts, dp = mesh.shape["expert"], mesh.shape["dp"]
    x_size = y_size = 4
    z_size = experts // (x_size * y_size)
    grid = Mesh(mesh.devices.reshape(x_size, z_size, y_size, dp), ("x", "z", "y", "dp"))
    every, owner = ("x", "z", "y", "dp"), ("x", "z", "y")
    return jax.shard_map(
        body,
        mesh=grid,
        in_specs=(
            P(every, None),
            P(every, None),
            P(every, None),
            P(owner, None, "dp"),
            P(owner, None, "dp"),
            P(owner, "dp", None),
        ),
        out_specs=P(every, None),
        check_vma=False,
    )
```

```python
import functools

import jax
import jax.numpy as jnp
import numpy as np
from jax import lax
from jax.experimental import pallas as pl
from jax.experimental.pallas import tpu as pltpu
from jax.sharding import Mesh
from jax.sharding import PartitionSpec as P

GROUP = 4
DEPTH = 512
ARRIVE = (1536, 2560)
LEAVE = (2048, 2048)


def slot_table(routes, gate_probs, sizes, capacity):
    x_size, z_size, y_size = sizes
    tok_count, top_count = routes.shape
    flat = routes.T.reshape(-1)
    token = jnp.arange(tok_count * top_count, dtype=jnp.int32) % tok_count
    earlier = (flat[:, None] == flat[None, :]) & (token[None, :] < token[:, None])
    slot = jnp.sum(earlier.astype(jnp.int32), axis=1)
    ex, ez, ey = flat // (z_size * y_size), flat // y_size % z_size, flat % y_size
    target = ((ez * x_size + ex) * y_size + ey) * capacity + slot
    slots = jnp.arange(x_size * z_size * y_size * capacity, dtype=jnp.int32)
    here = target[None, :] == slots[:, None]
    held = jnp.sum(jnp.where(here, (token + 1).astype(jnp.float32)[None, :], 0.0), axis=1)
    prob = jnp.sum(jnp.where(here, gate_probs.T.reshape(-1)[None, :], 0.0), axis=1)
    high = lax.reduce_precision(prob, 8, 7)
    table = jnp.stack([held, high, prob - high]).reshape(3, z_size, -1)
    return table.transpose(1, 0, 2).astype(jnp.bfloat16)


def hits(table_ref, i, tok_count):
    row_token = table_ref[i, 0:1, :].astype(jnp.float32).astype(jnp.int32) - 1
    lanes = row_token.shape[1]
    return lax.broadcasted_iota(jnp.int32, (tok_count, lanes), 0) == row_token


def pack_kernel(table_ref, tok_ref, _, out_ref):
    plane, sources, capacity, width = out_ref.shape
    for i in range(sources):
        block = tok_ref[i]
        place = jnp.where(hits(table_ref, i, block.shape[0]), 1.0, 0.0).astype(jnp.bfloat16)
        rows = lax.dot_general(
            place, block, (((0,), (0,)), ((), ())), preferred_element_type=jnp.float32
        )
        out_ref[:, i] = rows.astype(jnp.bfloat16).reshape(plane, capacity, width)


def pack(table, tok, after, tok_count, plane, capacity):
    sources, _, width = tok.shape
    return pl.pallas_call(
        pack_kernel,
        grid=(sources // GROUP,),
        in_specs=[
            pl.BlockSpec((GROUP,) + table.shape[1:], lambda i: (i, 0, 0)),
            pl.BlockSpec((GROUP, tok_count, width), lambda i: (i, 0, 0)),
            pl.BlockSpec(after.shape, lambda i: (0, 0)),
        ],
        out_specs=pl.BlockSpec((plane, GROUP, capacity, width), lambda i: (0, i, 0, 0)),
        out_shape=jax.ShapeDtypeStruct((plane, sources, capacity, width), tok.dtype),
        name="pack",
    )(table, tok, after)


def mix_kernel(table_ref, rows_ref, out_ref):
    plane, sources, capacity, width = rows_ref.shape
    tok_count = out_ref.shape[1]
    for i in range(sources):
        here = hits(table_ref, i, tok_count)
        both = [
            jnp.where(here, table_ref[i, r : r + 1, :].astype(jnp.float32), 0.0) for r in (1, 2)
        ]
        both = jnp.concatenate(both, axis=0).astype(jnp.bfloat16)
        rows = rows_ref[:, i].reshape(plane * capacity, width)
        sums = jnp.dot(both, rows, preferred_element_type=jnp.float32)
        out_ref[i] = (sums[:tok_count] + sums[tok_count:]).astype(out_ref.dtype)


def mix(table, rows, tok_count):
    plane, sources, capacity, width = rows.shape
    return pl.pallas_call(
        mix_kernel,
        grid=(sources // GROUP,),
        in_specs=[
            pl.BlockSpec((GROUP,) + table.shape[1:], lambda i: (i, 0, 0)),
            pl.BlockSpec((plane, GROUP, capacity, width), lambda i: (0, i, 0, 0)),
        ],
        out_specs=pl.BlockSpec((GROUP, tok_count, width), lambda i: (i, 0, 0)),
        out_shape=jax.ShapeDtypeStruct((sources, tok_count, width), jnp.bfloat16),
        name="mix",
    )(table, rows)


def hidden_kernel(first_ref, second_ref, gate_ref, up_ref, out_ref, gate_acc, up_acc, *, split):
    step, steps = pl.program_id(0), pl.num_programs(0)

    def products(rows_ref):
        return dot(rows_ref[...], gate_ref[...]), dot(rows_ref[...], up_ref[...])

    @pl.when(step == 0)
    def _():
        gate_acc[...], up_acc[...] = products(first_ref)

    @pl.when((step > 0) & (step < split))
    def _():
        gate, up = products(first_ref)
        gate_acc[...] += gate
        up_acc[...] += up

    @pl.when((step >= split) & (step < steps - 1))
    def _():
        gate, up = products(second_ref)
        gate_acc[...] += gate
        up_acc[...] += up

    @pl.when(step == steps - 1)
    def _():
        gate, up = products(second_ref)
        out_ref[...] = (jax.nn.silu(gate_acc[...] + gate) * (up_acc[...] + up)).astype(out_ref.dtype)


def hidden_of(first, second, w_gate, w_up):
    count = first.shape[0]
    depth, units = w_gate.shape
    split = first.shape[1] // DEPTH
    weight = pl.BlockSpec((DEPTH, units), lambda i: (i, 0))
    return pl.pallas_call(
        functools.partial(hidden_kernel, split=split),
        grid=(depth // DEPTH,),
        in_specs=[
            pl.BlockSpec((count, DEPTH), lambda i: (0, jnp.minimum(i, split - 1))),
            pl.BlockSpec((count, DEPTH), lambda i: (0, jnp.maximum(i - split, 0))),
            weight,
            weight,
        ],
        out_specs=pl.BlockSpec((count, units), lambda i: (0, 0)),
        out_shape=jax.ShapeDtypeStruct((count, units), jnp.bfloat16),
        scratch_shapes=[pltpu.VMEM((count, units), jnp.float32)] * 2,
        compiler_params=pltpu.CompilerParams(vmem_limit_bytes=56 << 20),
        name="hidden",
    )(first, second, w_gate, w_up)


def cuts(widths):
    ends = np.cumsum(widths)
    return [slice(int(end) - width, int(end)) for width, end in zip(widths, ends, strict=True)]


def dot(a, b):
    return jnp.dot(a, b, preferred_element_type=jnp.float32)


def body(tokens, routes, gate_probs, gate_w, up_w, down_w):
    sizes = tuple(lax.axis_size(a) for a in ("x", "z", "y"))
    x_size, z_size, y_size = sizes
    plane = x_size * y_size
    tok_count, model_width = tokens.shape
    capacity = 2 * tok_count * routes.shape[1] // (plane * z_size)
    rows_here = plane * z_size * capacity
    my_z = lax.axis_index("z")

    def in_plane(rows):
        width = rows.shape[-1]
        rows = rows.reshape(plane, z_size * capacity, width)
        rows = lax.all_to_all(rows, ("x", "y"), split_axis=0, concat_axis=0, tiled=True)
        return rows.reshape(plane, z_size, capacity, width)

    into, back = cuts(ARRIVE), cuts(LEAVE)
    table = slot_table(routes, gate_probs, sizes, capacity).reshape(z_size, -1)
    table = jnp.pad(table, ((0, 0), (0, ARRIVE[0] - table.shape[1])))
    sent = [jnp.concatenate([tokens[:, into[0]], table], axis=0), tokens[:, into[1]]]
    gathered = [lax.all_gather(part, "z", axis=0, tiled=False) for part in sent]

    swap = [(0, 1), (1, 0)]

    def whole(w, axis):
        return jnp.concatenate([w, lax.ppermute(w, "dp", swap)], axis=axis)

    w_gate, w_up, w_down = whole(gate_w[0], 1), whole(up_w[0], 1), whole(down_w[0], 0)

    first, second = gathered
    w_gate, w_up, w_down, first = lax.optimization_barrier((w_gate, w_up, w_down, first))
    table = lax.dynamic_index_in_dim(first, tok_count + my_z, 1, keepdims=False)
    table = table[:, : 3 * plane * capacity].reshape(z_size, 3, plane * capacity)
    arrived, after = [], jnp.zeros((8, 128), tokens.dtype)
    for block in (first, second):
        rows = in_plane(pack(table, block, after, tok_count, plane, capacity))
        arrived.append(rows.reshape(rows_here, -1))
        after = arrived[-1][:8, :128] + 1
    hidden = hidden_of(*arrived, w_gate, w_up)

    outs = []
    for part in back:
        answers = dot(hidden, w_down[:, part]).astype(jnp.bfloat16)
        rows = in_plane(answers.reshape(plane, z_size, capacity, -1))
        partial = mix(table, rows, tok_count)
        partial, hidden = lax.optimization_barrier((partial, hidden))
        outs.append(lax.psum_scatter(partial, "z", scatter_dimension=0, tiled=True)[0])
    return jnp.concatenate(outs, axis=1)


def solution(mesh):
    experts, dp = mesh.shape["expert"], mesh.shape["dp"]
    x_size = y_size = 4
    z_size = experts // (x_size * y_size)
    grid = Mesh(mesh.devices.reshape(x_size, z_size, y_size, dp), ("x", "z", "y", "dp"))
    every, owner = ("x", "z", "y", "dp"), ("x", "z", "y")
    return jax.shard_map(
        body,
        mesh=grid,
        in_specs=(
            P(every, None),
            P(every, None),
            P(every, None),
            P(owner, None, "dp"),
            P(owner, None, "dp"),
            P(owner, "dp", None),
        ),
        out_specs=P(every, None),
        check_vma=False,
    )
```

```python
import functools

import jax
import jax.numpy as jnp
import numpy as np
from jax import lax
from jax.experimental import pallas as pl
from jax.experimental.pallas import tpu as pltpu
from jax.sharding import Mesh
from jax.sharding import PartitionSpec as P

DEPTH = 1024
ARRIVE = (1024, 3072)
LEAVE = (3328, 768)


def slot_table(routes, gate_probs, sizes, capacity):
    x_size, z_size, y_size = sizes
    tok_count, top_count = routes.shape
    flat = routes.T.reshape(-1)
    token = jnp.arange(tok_count * top_count, dtype=jnp.int32) % tok_count
    earlier = (flat[:, None] == flat[None, :]) & (token[None, :] < token[:, None])
    slot = jnp.sum(earlier.astype(jnp.int32), axis=1)
    ex, ez, ey = flat // (z_size * y_size), flat // y_size % z_size, flat % y_size
    target = ((ez * x_size + ex) * y_size + ey) * capacity + slot
    slots = jnp.arange(x_size * z_size * y_size * capacity, dtype=jnp.int32)
    here = target[None, :] == slots[:, None]
    held = jnp.sum(jnp.where(here, (token + 1).astype(jnp.float32)[None, :], 0.0), axis=1)
    prob = jnp.sum(jnp.where(here, gate_probs.T.reshape(-1)[None, :], 0.0), axis=1)
    high = lax.reduce_precision(prob, 8, 7)
    table = jnp.stack([held, high, prob - high]).reshape(3, z_size, -1)
    return table.transpose(1, 0, 2).astype(jnp.bfloat16)


def hits(row_token, tok_count):
    tokens = lax.broadcasted_iota(jnp.int32, (tok_count, row_token.shape[1]), 0)
    return tokens == row_token.astype(jnp.int32) - 1


def place_rows(here, block):
    place = jnp.where(here, 1.0, 0.0).astype(jnp.bfloat16)
    rows = lax.dot_general(
        place, block, (((0,), (0,)), ((), ())), preferred_element_type=jnp.float32
    )
    return rows.astype(jnp.bfloat16)


def pack_ring_kernel(me_ref, *refs):
    *blocks, far_first, far_second, out_ref, table_ref = refs
    plane, sources, capacity, width = out_ref.shape
    lanes = plane * capacity
    tok_count = far_second.shape[0]
    for i in range(sources):
        ref = blocks[i] if i < len(blocks) else far_first
        lists = ref[tok_count:, : 3 * lanes].astype(jnp.float32)
        mine = lax.broadcasted_iota(jnp.int32, lists.shape, 0) == me_ref[0]
        lists = jnp.sum(jnp.where(mine, lists, 0.0), axis=0, keepdims=True)
        for r in range(3):
            table_ref[i, r : r + 1, :] = lists[:, r * lanes : (r + 1) * lanes]
        here = hits(lists[:, :lanes], tok_count)
        if i < len(blocks):
            rows = place_rows(here, ref[:tok_count, :])
            out_ref[:, i] = rows.reshape(plane, capacity, width)
        else:
            half = width // 2
            rows = place_rows(here, far_first[:tok_count, :])
            out_ref[:, i, :, :half] = rows.reshape(plane, capacity, half)
            rows = place_rows(here, far_second[...])
            out_ref[:, i, :, half:] = rows.reshape(plane, capacity, half)


def pack_ring(me, blocks, tok_count, plane, capacity):
    sources, width = len(blocks) - 1, blocks[0].shape[1]
    whole = [pl.BlockSpec(b.shape, lambda i, me: (0, 0)) for b in blocks]
    shapes = [(plane, sources, capacity, width), (sources, 3, plane * capacity)]
    return pl.pallas_call(
        pack_ring_kernel,
        grid_spec=pltpu.PrefetchScalarGridSpec(
            num_scalar_prefetch=1,
            grid=(1,),
            in_specs=whole,
            out_specs=[
                pl.BlockSpec(shapes[0], lambda i, me: (0, 0, 0, 0)),
                pl.BlockSpec(shapes[1], lambda i, me: (0, 0, 0)),
            ],
        ),
        out_shape=[
            jax.ShapeDtypeStruct(shapes[0], jnp.bfloat16),
            jax.ShapeDtypeStruct(shapes[1], jnp.float32),
        ],
        name="pack_ring",
    )(me, *blocks)


def pack_kernel(order_ref, table_ref, tok_ref, _, out_ref):
    plane, sources, capacity, width = out_ref.shape
    for i in range(sources):
        here = hits(table_ref[i, 0:1, :], tok_ref.shape[1])
        rows = place_rows(here, tok_ref[order_ref[i]])
        out_ref[:, i] = rows.reshape(plane, capacity, width)


def pack(order, table, tok, after, plane, capacity, step):
    sources, tok_count, width = tok.shape
    return pl.pallas_call(
        pack_kernel,
        grid_spec=pltpu.PrefetchScalarGridSpec(
            num_scalar_prefetch=1,
            grid=(width // step,),
            in_specs=[
                pl.BlockSpec(table.shape, lambda i, order: (0, 0, 0)),
                pl.BlockSpec((sources, tok_count, step), lambda i, order: (0, 0, i)),
                pl.BlockSpec(after.shape, lambda i, order: (0, 0)),
            ],
            out_specs=pl.BlockSpec((plane, sources, capacity, step), lambda i, order: (0, 0, 0, i)),
        ),
        out_shape=jax.ShapeDtypeStruct((plane, sources, capacity, width), tok.dtype),
        name="pack",
    )(order, table, tok, after)


def mix_kernel(order_ref, table_ref, rows_ref, out_ref):
    plane, sources, capacity, width = rows_ref.shape
    tok_count = out_ref.shape[1]
    for i in range(sources):
        here = hits(table_ref[i, 0:1, :], tok_count)
        both = [jnp.where(here, table_ref[i, r : r + 1, :], 0.0) for r in (1, 2)]
        both = jnp.concatenate(both, axis=0).astype(jnp.bfloat16)
        rows = rows_ref[:, i].reshape(plane * capacity, width)
        sums = jnp.dot(both, rows, preferred_element_type=jnp.float32)
        out_ref[order_ref[i]] = (sums[:tok_count] + sums[tok_count:]).astype(out_ref.dtype)


def mix(order, table, rows, tok_count, step):
    plane, sources, capacity, width = rows.shape
    return pl.pallas_call(
        mix_kernel,
        grid_spec=pltpu.PrefetchScalarGridSpec(
            num_scalar_prefetch=1,
            grid=(width // step,),
            in_specs=[
                pl.BlockSpec(table.shape, lambda i, order: (0, 0, 0)),
                pl.BlockSpec((plane, sources, capacity, step), lambda i, order: (0, 0, 0, i)),
            ],
            out_specs=pl.BlockSpec((sources, tok_count, step), lambda i, order: (0, 0, i)),
        ),
        out_shape=jax.ShapeDtypeStruct((sources, tok_count, width), jnp.bfloat16),
        name="mix",
    )(order, table, rows)


def hidden_kernel(first_ref, second_ref, *refs, split):
    *weights, out_ref, gate_acc, up_acc = refs
    step, steps = pl.program_id(0), pl.num_programs(0)

    def products(rows_ref):
        gate, gate_other, up, up_other = (ref[...] for ref in weights)
        gate = jnp.concatenate([gate, gate_other], axis=1)
        up = jnp.concatenate([up, up_other], axis=1)
        return dot(rows_ref[...], gate), dot(rows_ref[...], up)

    @pl.when(step == 0)
    def _():
        gate_acc[...], up_acc[...] = products(first_ref)

    if split > 1:

        @pl.when((step > 0) & (step < split))
        def _():
            gate, up = products(first_ref)
            gate_acc[...] += gate
            up_acc[...] += up

    @pl.when((step >= split) & (step < steps - 1))
    def _():
        gate, up = products(second_ref)
        gate_acc[...] += gate
        up_acc[...] += up

    @pl.when(step == steps - 1)
    def _():
        gate, up = products(second_ref)
        out_ref[...] = (jax.nn.silu(gate_acc[...] + gate) * (up_acc[...] + up)).astype(out_ref.dtype)


def hidden_of(first, second, weights):
    count = first.shape[0]
    depth, units = weights[0].shape
    split = first.shape[1] // DEPTH
    weight = pl.BlockSpec((DEPTH, units), lambda i: (i, 0))
    return pl.pallas_call(
        functools.partial(hidden_kernel, split=split),
        grid=(depth // DEPTH,),
        in_specs=[
            pl.BlockSpec((count, DEPTH), lambda i: (0, jnp.minimum(i, split - 1))),
            pl.BlockSpec((count, DEPTH), lambda i: (0, jnp.maximum(i - split, 0))),
            *[weight] * 4,
        ],
        out_specs=pl.BlockSpec((count, 2 * units), lambda i: (0, 0)),
        out_shape=jax.ShapeDtypeStruct((count, 2 * units), jnp.bfloat16),
        scratch_shapes=[pltpu.VMEM((count, 2 * units), jnp.float32)] * 2,
        compiler_params=pltpu.CompilerParams(vmem_limit_bytes=56 << 20),
        name="hidden",
    )(first, second, *weights)


def cuts(widths):
    ends = np.cumsum(widths)
    return [slice(int(end) - width, int(end)) for width, end in zip(widths, ends, strict=True)]


def dot(a, b):
    return jnp.dot(a, b, preferred_element_type=jnp.float32)


def body(tokens, routes, gate_probs, gate_w, up_w, down_w):
    sizes = tuple(lax.axis_size(a) for a in ("x", "z", "y"))
    x_size, z_size, y_size = sizes
    plane = x_size * y_size
    tok_count, model_width = tokens.shape
    capacity = 2 * tok_count * routes.shape[1] // (plane * z_size)
    rows_here = plane * z_size * capacity
    my_z = lax.axis_index("z")

    def in_plane(rows):
        width = rows.shape[-1]
        rows = rows.reshape(plane, z_size * capacity, width)
        rows = lax.all_to_all(rows, ("x", "y"), split_axis=0, concat_axis=0, tiled=True)
        return rows.reshape(plane, z_size, capacity, width)

    into, back = cuts(ARRIVE), cuts(LEAVE)
    up_ring = [(i, (i + 1) % z_size) for i in range(z_size)]
    down_ring = [(i, (i - 1) % z_size) for i in range(z_size)]

    second = lax.all_gather(tokens[:, into[1]], "z", axis=0, tiled=False)

    table = slot_table(routes, gate_probs, sizes, capacity).reshape(z_size, -1)
    table = jnp.pad(table, ((0, 0), (0, ARRIVE[0] - table.shape[1])))
    above = below = jnp.concatenate([tokens[:, into[0]], table], axis=0)
    ring, order = [above], [my_z]
    for hop in range(1, z_size // 2):
        above, below = lax.ppermute(above, "z", up_ring), lax.ppermute(below, "z", down_ring)
        ring += [above, below]
        order += [my_z - hop, my_z + hop]
    half = ARRIVE[0] // 2
    ring.append(lax.ppermute(above[:, :half], "z", up_ring))
    ring.append(lax.ppermute(below[:tok_count, half:], "z", down_ring))
    order = jnp.stack([*order, my_z + z_size // 2]) % z_size

    swap = [(0, 1), (1, 0)]
    weights = [gate_w[0], up_w[0]]
    weights = [v for w in weights for v in (w, lax.ppermute(w, "dp", swap))]
    w_down = jnp.concatenate([down_w[0], lax.ppermute(down_w[0], "dp", swap)], axis=0)

    weights, w_down, ring, order = lax.optimization_barrier((weights, w_down, ring, order))
    rows, table = pack_ring(my_z[None], ring, tok_count, plane, capacity)
    rows = in_plane(rows)
    first = rows.reshape(rows_here, -1)
    after = first[:8, :128] + 1
    rows = in_plane(pack(order, table, second, after, plane, capacity, ARRIVE[1] // 3))
    hidden = hidden_of(first, rows.reshape(rows_here, -1), weights)

    def answered(hidden, part, step):
        answers = dot(hidden, w_down[:, part]).astype(jnp.bfloat16)
        rows = in_plane(answers.reshape(plane, z_size, capacity, -1))
        return mix(order, table, rows, tok_count, step)

    partial = answered(hidden, back[0], LEAVE[0] // 2)
    partial, hidden = lax.optimization_barrier((partial, hidden))
    out_first = lax.psum_scatter(partial, "z", scatter_dimension=0, tiled=True)[0]
    partial = answered(hidden, back[1], LEAVE[1])
    parts = lax.all_to_all(partial, "z", split_axis=0, concat_axis=0, tiled=True)
    out_second = jnp.sum(parts.astype(jnp.float32), axis=0).astype(jnp.bfloat16)
    return jnp.concatenate([out_first, out_second], axis=1)


def solution(mesh):
    experts, dp = mesh.shape["expert"], mesh.shape["dp"]
    x_size = y_size = 4
    z_size = experts // (x_size * y_size)
    grid = Mesh(mesh.devices.reshape(x_size, z_size, y_size, dp), ("x", "z", "y", "dp"))
    every, owner = ("x", "z", "y", "dp"), ("x", "z", "y")
    return jax.shard_map(
        body,
        mesh=grid,
        in_specs=(
            P(every, None),
            P(every, None),
            P(every, None),
            P(owner, None, "dp"),
            P(owner, None, "dp"),
            P(owner, "dp", None),
        ),
        out_specs=P(every, None),
        check_vma=False,
    )
```

```python
import functools

import jax
import jax.numpy as jnp
import numpy as np
from jax import lax
from jax.experimental import pallas as pl
from jax.experimental.pallas import tpu as pltpu
from jax.sharding import Mesh
from jax.sharding import PartitionSpec as P

DEPTH = 512
ARRIVE = (512, 3584)
LEAVE = (3328, 768)


def slot_table(routes, gate_probs, sizes, capacity):
    x_size, z_size, y_size = sizes
    tok_count, top_count = routes.shape
    flat = routes.T.reshape(-1)
    token = jnp.arange(tok_count * top_count, dtype=jnp.int32) % tok_count
    earlier = (flat[:, None] == flat[None, :]) & (token[None, :] < token[:, None])
    slot = jnp.sum(earlier.astype(jnp.int32), axis=1)
    ex, ez, ey = flat // (z_size * y_size), flat // y_size % z_size, flat % y_size
    target = ((ez * x_size + ex) * y_size + ey) * capacity + slot
    slots = jnp.arange(x_size * z_size * y_size * capacity, dtype=jnp.int32)
    here = target[None, :] == slots[:, None]
    held = jnp.sum(jnp.where(here, (token + 1).astype(jnp.float32)[None, :], 0.0), axis=1)
    prob = jnp.sum(jnp.where(here, gate_probs.T.reshape(-1)[None, :], 0.0), axis=1)
    high = lax.reduce_precision(prob, 8, 7)
    table = jnp.stack([held, high, prob - high]).reshape(3, z_size, -1)
    return table.transpose(1, 0, 2).astype(jnp.bfloat16)


def hits(row_token, tok_count):
    tokens = lax.broadcasted_iota(jnp.int32, (tok_count, row_token.shape[1]), 0)
    return tokens == row_token.astype(jnp.int32) - 1


def place_rows(here, block):
    place = jnp.where(here, 1.0, 0.0).astype(jnp.bfloat16)
    rows = lax.dot_general(
        place, block, (((0,), (0,)), ((), ())), preferred_element_type=jnp.float32
    )
    return rows.astype(jnp.bfloat16)


def pack_ring_kernel(me_ref, *refs):
    *blocks, far_first, far_second, out_ref, table_ref = refs
    plane, sources, capacity, width = out_ref.shape
    lanes = plane * capacity
    tok_count = blocks[0].shape[0] - sources
    for i in range(sources):
        if i < len(blocks):
            block, lists = blocks[i][:tok_count, :], blocks[i][tok_count:, : 3 * lanes]
        else:
            half = tok_count - far_first.shape[0]
            block = jnp.concatenate([far_first[...], far_second[:half, :]], axis=0)
            lists = far_second[half:, : 3 * lanes]
        lists = lists.astype(jnp.float32)
        mine = lax.broadcasted_iota(jnp.int32, lists.shape, 0) == me_ref[0]
        lists = jnp.sum(jnp.where(mine, lists, 0.0), axis=0, keepdims=True)
        for r in range(3):
            table_ref[i, r : r + 1, :] = lists[:, r * lanes : (r + 1) * lanes]
        rows = place_rows(hits(lists[:, :lanes], tok_count), block)
        out_ref[:, i] = rows.reshape(plane, capacity, width)


def pack_ring(me, blocks, tok_count, plane, capacity):
    sources, width = len(blocks) - 1, blocks[0].shape[1]
    whole = [pl.BlockSpec(b.shape, lambda i, me: (0, 0)) for b in blocks]
    shapes = [(plane, sources, capacity, width), (sources, 3, plane * capacity)]
    return pl.pallas_call(
        pack_ring_kernel,
        grid_spec=pltpu.PrefetchScalarGridSpec(
            num_scalar_prefetch=1,
            grid=(1,),
            in_specs=whole,
            out_specs=[
                pl.BlockSpec(shapes[0], lambda i, me: (0, 0, 0, 0)),
                pl.BlockSpec(shapes[1], lambda i, me: (0, 0, 0)),
            ],
        ),
        out_shape=[
            jax.ShapeDtypeStruct(shapes[0], jnp.bfloat16),
            jax.ShapeDtypeStruct(shapes[1], jnp.float32),
        ],
        name="pack_ring",
    )(me, *blocks)


def pack_kernel(order_ref, table_ref, tok_ref, _, out_ref):
    plane, sources, capacity, width = out_ref.shape
    for i in range(sources):
        here = hits(table_ref[i, 0:1, :], tok_ref.shape[1])
        rows = place_rows(here, tok_ref[order_ref[i]])
        out_ref[:, i] = rows.reshape(plane, capacity, width)


def pack(order, table, tok, after, plane, capacity, step):
    sources, tok_count, width = tok.shape
    return pl.pallas_call(
        pack_kernel,
        grid_spec=pltpu.PrefetchScalarGridSpec(
            num_scalar_prefetch=1,
            grid=(width // step,),
            in_specs=[
                pl.BlockSpec(table.shape, lambda i, order: (0, 0, 0)),
                pl.BlockSpec((sources, tok_count, step), lambda i, order: (0, 0, i)),
                pl.BlockSpec(after.shape, lambda i, order: (0, 0)),
            ],
            out_specs=pl.BlockSpec((plane, sources, capacity, step), lambda i, order: (0, 0, 0, i)),
        ),
        out_shape=jax.ShapeDtypeStruct((plane, sources, capacity, width), tok.dtype),
        name="pack",
    )(order, table, tok, after)


def mix_kernel(order_ref, table_ref, rows_ref, out_ref):
    plane, sources, capacity, width = rows_ref.shape
    tok_count = out_ref.shape[1]
    for i in range(sources):
        here = hits(table_ref[i, 0:1, :], tok_count)
        both = [jnp.where(here, table_ref[i, r : r + 1, :], 0.0) for r in (1, 2)]
        both = jnp.concatenate(both, axis=0).astype(jnp.bfloat16)
        rows = rows_ref[:, i].reshape(plane * capacity, width)
        sums = jnp.dot(both, rows, preferred_element_type=jnp.float32)
        out_ref[order_ref[i]] = (sums[:tok_count] + sums[tok_count:]).astype(out_ref.dtype)


def mix(order, table, rows, tok_count, step):
    plane, sources, capacity, width = rows.shape
    return pl.pallas_call(
        mix_kernel,
        grid_spec=pltpu.PrefetchScalarGridSpec(
            num_scalar_prefetch=1,
            grid=(width // step,),
            in_specs=[
                pl.BlockSpec(table.shape, lambda i, order: (0, 0, 0)),
                pl.BlockSpec((plane, sources, capacity, step), lambda i, order: (0, 0, 0, i)),
            ],
            out_specs=pl.BlockSpec((sources, tok_count, step), lambda i, order: (0, 0, i)),
        ),
        out_shape=jax.ShapeDtypeStruct((sources, tok_count, width), jnp.bfloat16),
        name="mix",
    )(order, table, rows)


def hidden_kernel(first_ref, second_ref, *refs, split):
    *weights, out_ref, gate_acc, up_acc = refs
    step, steps = pl.program_id(0), pl.num_programs(0)

    def products(rows_ref):
        gate, gate_other, up, up_other = (ref[...] for ref in weights)
        gate = jnp.concatenate([gate, gate_other], axis=1)
        up = jnp.concatenate([up, up_other], axis=1)
        return dot(rows_ref[...], gate), dot(rows_ref[...], up)

    @pl.when(step == 0)
    def _():
        gate_acc[...], up_acc[...] = products(first_ref)

    if split > 1:

        @pl.when((step > 0) & (step < split))
        def _():
            gate, up = products(first_ref)
            gate_acc[...] += gate
            up_acc[...] += up

    @pl.when((step >= split) & (step < steps - 1))
    def _():
        gate, up = products(second_ref)
        gate_acc[...] += gate
        up_acc[...] += up

    @pl.when(step == steps - 1)
    def _():
        gate, up = products(second_ref)
        out_ref[...] = (jax.nn.silu(gate_acc[...] + gate) * (up_acc[...] + up)).astype(out_ref.dtype)


def hidden_of(first, second, weights):
    count = first.shape[0]
    depth, units = weights[0].shape
    split = first.shape[1] // DEPTH
    weight = pl.BlockSpec((DEPTH, units), lambda i: (i, 0))
    return pl.pallas_call(
        functools.partial(hidden_kernel, split=split),
        grid=(depth // DEPTH,),
        in_specs=[
            pl.BlockSpec((count, DEPTH), lambda i: (0, jnp.minimum(i, split - 1))),
            pl.BlockSpec((count, DEPTH), lambda i: (0, jnp.maximum(i - split, 0))),
            *[weight] * 4,
        ],
        out_specs=pl.BlockSpec((count, 2 * units), lambda i: (0, 0)),
        out_shape=jax.ShapeDtypeStruct((count, 2 * units), jnp.bfloat16),
        scratch_shapes=[pltpu.VMEM((count, 2 * units), jnp.float32)] * 2,
        compiler_params=pltpu.CompilerParams(vmem_limit_bytes=56 << 20),
        name="hidden",
    )(first, second, *weights)


def cuts(widths):
    ends = np.cumsum(widths)
    return [slice(int(end) - width, int(end)) for width, end in zip(widths, ends, strict=True)]


def dot(a, b):
    return jnp.dot(a, b, preferred_element_type=jnp.float32)


def body(tokens, routes, gate_probs, gate_w, up_w, down_w):
    sizes = tuple(lax.axis_size(a) for a in ("x", "z", "y"))
    x_size, z_size, y_size = sizes
    plane = x_size * y_size
    tok_count, model_width = tokens.shape
    capacity = 2 * tok_count * routes.shape[1] // (plane * z_size)
    rows_here = plane * z_size * capacity
    my_z = lax.axis_index("z")

    def in_plane(rows):
        width = rows.shape[-1]
        rows = rows.reshape(plane, z_size * capacity, width)
        rows = lax.all_to_all(rows, ("x", "y"), split_axis=0, concat_axis=0, tiled=True)
        return rows.reshape(plane, z_size, capacity, width)

    into, back = cuts(ARRIVE), cuts(LEAVE)
    up_ring = [(i, (i + 1) % z_size) for i in range(z_size)]
    down_ring = [(i, (i - 1) % z_size) for i in range(z_size)]

    second = lax.all_gather(tokens[:, into[1]], "z", axis=0, tiled=False)

    table = slot_table(routes, gate_probs, sizes, capacity).reshape(z_size, -1)
    table = jnp.pad(table, ((0, 0), (0, ARRIVE[0] - table.shape[1])))
    above = below = jnp.concatenate([tokens[:, into[0]], table], axis=0)
    ring, order = [above], [my_z]
    for hop in range(1, z_size // 2):
        above, below = lax.ppermute(above, "z", up_ring), lax.ppermute(below, "z", down_ring)
        ring += [above, below]
        order += [my_z - hop, my_z + hop]
    half = tok_count // 2
    ring.append(lax.ppermute(below[:half], "z", down_ring))
    ring.append(lax.ppermute(above[half:], "z", up_ring))
    order = jnp.stack([*order, my_z + z_size // 2]) % z_size

    swap = [(0, 1), (1, 0)]
    weights = [gate_w[0], up_w[0]]
    weights = [v for w in weights for v in (w, lax.ppermute(w, "dp", swap))]
    down_other = lax.ppermute(down_w[0], "dp", swap)

    weights, down_other, ring, order = lax.optimization_barrier((weights, down_other, ring, order))
    rows, table = pack_ring(my_z[None], ring, tok_count, plane, capacity)
    rows = in_plane(rows)
    first = rows.reshape(rows_here, -1)
    after, down_other = lax.optimization_barrier((first[:8, :128] + 1, down_other))
    w_down = jnp.concatenate([down_w[0], down_other], axis=0)
    after, w_down = lax.optimization_barrier((after, w_down))
    rows = in_plane(pack(order, table, second, after, plane, capacity, ARRIVE[1] // 4))
    hidden = hidden_of(first, rows.reshape(rows_here, -1), weights)

    def answered(hidden, part, step):
        answers = dot(hidden, w_down[:, part]).astype(jnp.bfloat16)
        rows = in_plane(answers.reshape(plane, z_size, capacity, -1))
        return mix(order, table, rows, tok_count, step)

    partial = answered(hidden, back[0], LEAVE[0] // 2)
    partial, hidden = lax.optimization_barrier((partial, hidden))
    out_first = lax.psum_scatter(partial, "z", scatter_dimension=0, tiled=True)[0]
    partial = answered(hidden, back[1], LEAVE[1])
    parts = lax.all_to_all(partial, "z", split_axis=0, concat_axis=0, tiled=True)
    out_second = jnp.sum(parts.astype(jnp.float32), axis=0).astype(jnp.bfloat16)
    return jnp.concatenate([out_first, out_second], axis=1)


def solution(mesh):
    experts, dp = mesh.shape["expert"], mesh.shape["dp"]
    x_size = y_size = 4
    z_size = experts // (x_size * y_size)
    grid = Mesh(mesh.devices.reshape(x_size, z_size, y_size, dp), ("x", "z", "y", "dp"))
    every, owner = ("x", "z", "y", "dp"), ("x", "z", "y")
    return jax.shard_map(
        body,
        mesh=grid,
        in_specs=(
            P(every, None),
            P(every, None),
            P(every, None),
            P(owner, None, "dp"),
            P(owner, None, "dp"),
            P(owner, "dp", None),
        ),
        out_specs=P(every, None),
        check_vma=False,
    )
```

```python
import functools

import jax
import jax.numpy as jnp
import numpy as np
from jax import lax
from jax.experimental import pallas as pl
from jax.experimental.pallas import tpu as pltpu
from jax.sharding import Mesh
from jax.sharding import PartitionSpec as P

DEPTH = 512
STEP = 1024
LISTS = 512
NEAR = (0, -1, 1)


def slot_table(routes, gate_probs, sizes, capacity):
    x_size, z_size, y_size = sizes
    tok_count, top_count = routes.shape
    flat = routes.T.reshape(-1)
    token = jnp.arange(tok_count * top_count, dtype=jnp.int32) % tok_count
    earlier = (flat[:, None] == flat[None, :]) & (token[None, :] < token[:, None])
    slot = jnp.sum(earlier.astype(jnp.int32), axis=1)
    ex, ez, ey = flat // (z_size * y_size), flat // y_size % z_size, flat % y_size
    target = ((ez * x_size + ex) * y_size + ey) * capacity + slot
    slots = jnp.arange(x_size * z_size * y_size * capacity, dtype=jnp.int32)
    here = target[None, :] == slots[:, None]
    held = jnp.sum(jnp.where(here, (token + 1).astype(jnp.float32)[None, :], 0.0), axis=1)
    prob = jnp.sum(jnp.where(here, gate_probs.T.reshape(-1)[None, :], 0.0), axis=1)
    high = lax.reduce_precision(prob, 8, 7)
    table = jnp.stack([held, high, prob - high]).reshape(3, z_size, -1)
    return table.transpose(1, 0, 2).astype(jnp.bfloat16)


def hits(row_token, tok_count):
    tokens = lax.broadcasted_iota(jnp.int32, (tok_count, row_token.shape[1]), 0)
    return tokens == row_token.astype(jnp.int32) - 1


def place_rows(here, block):
    place = jnp.where(here, 1.0, 0.0).astype(jnp.bfloat16)
    rows = lax.dot_general(
        place, block, (((0,), (0,)), ((), ())), preferred_element_type=jnp.float32
    )
    return rows.astype(jnp.bfloat16)


def lists_of(rows, me, lanes):
    rows = rows[:, : 3 * lanes].astype(jnp.float32)
    mine = lax.broadcasted_iota(jnp.int32, rows.shape, 0) == me
    rows = jnp.sum(jnp.where(mine, rows, 0.0), axis=0, keepdims=True)
    return [rows[:, r * lanes : (r + 1) * lanes] for r in range(3)]


def mixed(lists, rows, tok_count):
    here = hits(lists[0], tok_count)
    both = jnp.concatenate([jnp.where(here, part, 0.0) for part in lists[1:]], axis=0)
    sums = jnp.dot(both.astype(jnp.bfloat16), rows, preferred_element_type=jnp.float32)
    return sums[:tok_count] + sums[tok_count:]


def pack_near_kernel(order_ref, *refs):
    *list_refs, out_ref = refs
    count = len(list_refs) // 2
    plane, _, capacity, width = out_ref.shape
    for i in range(count):
        token_ref = list_refs[count + i]
        lists = lists_of(list_refs[i][...], order_ref[0], plane * capacity)
        rows = place_rows(hits(lists[0], token_ref.shape[0]), token_ref[...])
        out_ref[:, i] = rows.reshape(plane, capacity, width)


def pack_near(order, blocks, tok_count, plane, capacity):
    count, width = len(blocks), blocks[0].shape[1]
    z_size = blocks[0].shape[0] - tok_count
    below = pl.BlockSpec((z_size, LISTS), lambda i, order: (tok_count // z_size, 0))
    return pl.pallas_call(
        pack_near_kernel,
        grid_spec=pltpu.PrefetchScalarGridSpec(
            num_scalar_prefetch=1,
            grid=(width // STEP,),
            in_specs=[below] * count
            + [pl.BlockSpec((tok_count, STEP), lambda i, order: (0, i))] * count,
            out_specs=pl.BlockSpec((plane, count, capacity, STEP), lambda i, order: (0, 0, 0, i)),
        ),
        out_shape=jax.ShapeDtypeStruct((plane, count, capacity, width), jnp.bfloat16),
        name="pack_near",
    )(order, *blocks, *blocks)


def pack_far_kernel(order_ref, lists_ref, tok_ref, _, out_ref):
    plane, count, capacity, width = out_ref.shape
    for i in range(count):
        src = order_ref[len(NEAR) + i]
        lists = lists_of(lists_ref[src], order_ref[0], plane * capacity)
        rows = place_rows(hits(lists[0], tok_ref.shape[1]), tok_ref[src])
        out_ref[:, i] = rows.reshape(plane, capacity, width)


def pack_far(order, blocks, after, tok_count, plane, capacity):
    z_size, _, width = blocks.shape
    count = z_size - len(NEAR)
    return pl.pallas_call(
        pack_far_kernel,
        grid_spec=pltpu.PrefetchScalarGridSpec(
            num_scalar_prefetch=1,
            grid=(width // STEP,),
            in_specs=[
                pl.BlockSpec((z_size, z_size, LISTS), lambda i, order: (0, tok_count // z_size, 0)),
                pl.BlockSpec((z_size, tok_count, STEP), lambda i, order: (0, 0, i)),
                pl.BlockSpec(after.shape, lambda i, order: (0, 0)),
            ],
            out_specs=pl.BlockSpec((plane, count, capacity, STEP), lambda i, order: (0, 0, 0, i)),
        ),
        out_shape=jax.ShapeDtypeStruct((plane, count, capacity, width), jnp.bfloat16),
        name="pack_far",
    )(order, blocks, blocks, after)


def mix_far_kernel(order_ref, lists_ref, rows_ref, out_ref):
    plane, count, capacity, width = rows_ref.shape
    for i in range(len(NEAR)):
        out_ref[order_ref[i]] = jnp.zeros(out_ref.shape[1:], out_ref.dtype)
    for i in range(count):
        src = order_ref[len(NEAR) + i]
        lists = lists_of(lists_ref[src], order_ref[0], plane * capacity)
        rows = rows_ref[:, i].reshape(plane * capacity, width)
        out_ref[src] = mixed(lists, rows, out_ref.shape[1]).astype(out_ref.dtype)


def mix_far(order, blocks, rows, tok_count):
    plane, count, capacity, width = rows.shape
    z_size = blocks.shape[0]
    return pl.pallas_call(
        mix_far_kernel,
        grid_spec=pltpu.PrefetchScalarGridSpec(
            num_scalar_prefetch=1,
            grid=(width // STEP,),
            in_specs=[
                pl.BlockSpec((z_size, z_size, LISTS), lambda i, order: (0, tok_count // z_size, 0)),
                pl.BlockSpec((plane, count, capacity, STEP), lambda i, order: (0, 0, 0, i)),
            ],
            out_specs=pl.BlockSpec((z_size, tok_count, STEP), lambda i, order: (0, 0, i)),
        ),
        out_shape=jax.ShapeDtypeStruct((z_size, tok_count, width), jnp.bfloat16),
        name="mix_far",
    )(order, blocks, rows)


def mix_near_kernel(order_ref, *refs):
    count = len(NEAR)
    rows_ref, outs = refs[count], refs[count + 1 :]
    plane, _, capacity, width = rows_ref.shape
    for i in range(count):
        lists = lists_of(refs[i][...], order_ref[0], plane * capacity)
        rows = rows_ref[:, i].reshape(plane * capacity, width)
        outs[i][...] = mixed(lists, rows, outs[i].shape[0]).astype(outs[i].dtype)


def mix_near(order, blocks, rows, tok_count):
    plane, count, capacity, width = rows.shape
    z_size = blocks[0].shape[0] - tok_count
    kinds = [jnp.bfloat16 if offset else jnp.float32 for offset in NEAR]
    return pl.pallas_call(
        mix_near_kernel,
        grid_spec=pltpu.PrefetchScalarGridSpec(
            num_scalar_prefetch=1,
            grid=(width // STEP,),
            in_specs=[pl.BlockSpec((z_size, LISTS), lambda i, order: (tok_count // z_size, 0))]
            * count
            + [pl.BlockSpec((plane, count, capacity, STEP), lambda i, order: (0, 0, 0, i))],
            out_specs=[pl.BlockSpec((tok_count, STEP), lambda i, order: (0, i))] * count,
        ),
        out_shape=[jax.ShapeDtypeStruct((tok_count, width), kind) for kind in kinds],
        name="mix_near",
    )(order, *blocks, rows)


def hidden_kernel(near_ref, far_ref, *refs):
    *weights, out_near, out_far, gate_near, up_near, gate_far, up_far = refs
    step, steps = pl.program_id(0), pl.num_programs(0)
    gate, gate_other, up, up_other = (ref[...] for ref in weights)
    gate = jnp.concatenate([gate, gate_other], axis=1)
    up = jnp.concatenate([up, up_other], axis=1)
    parts = [(near_ref, out_near, gate_near, up_near), (far_ref, out_far, gate_far, up_far)]
    for rows_ref, out_ref, gate_acc, up_acc in parts:
        rows = rows_ref[...]

        @pl.when(step == 0)
        def _():
            gate_acc[...] = dot(rows, gate)
            up_acc[...] = dot(rows, up)

        @pl.when((step > 0) & (step < steps - 1))
        def _():
            gate_acc[...] += dot(rows, gate)
            up_acc[...] += dot(rows, up)

        @pl.when(step == steps - 1)
        def _():
            gate_act = gate_acc[...] + dot(rows, gate)
            up_act = up_acc[...] + dot(rows, up)
            out_ref[...] = (jax.nn.silu(gate_act) * up_act).astype(out_ref.dtype)


def hidden_of(near, far, weights):
    depth, units = weights[0].shape
    counts = [near.shape[0], far.shape[0]]
    return pl.pallas_call(
        hidden_kernel,
        grid=(depth // DEPTH,),
        in_specs=[pl.BlockSpec((c, DEPTH), lambda i: (0, i)) for c in counts]
        + [pl.BlockSpec((DEPTH, units), lambda i: (i, 0))] * 4,
        out_specs=[pl.BlockSpec((c, 2 * units), lambda i: (0, 0)) for c in counts],
        out_shape=[jax.ShapeDtypeStruct((c, 2 * units), jnp.bfloat16) for c in counts],
        scratch_shapes=[pltpu.VMEM((c, 2 * units), jnp.float32) for c in counts for _ in range(2)],
        compiler_params=pltpu.CompilerParams(vmem_limit_bytes=56 << 20),
        name="hidden",
    )(near, far, *weights)


def dot(a, b):
    return jnp.dot(a, b, preferred_element_type=jnp.float32)


def body(tokens, routes, gate_probs, gate_w, up_w, down_w):
    sizes = tuple(lax.axis_size(a) for a in ("x", "z", "y"))
    x_size, z_size, y_size = sizes
    plane = x_size * y_size
    tok_count, model_width = tokens.shape
    capacity = 2 * tok_count * routes.shape[1] // (plane * z_size)
    my_z = lax.axis_index("z")
    up_ring = [(i, (i + 1) % z_size) for i in range(z_size)]
    down_ring = [(i, (i - 1) % z_size) for i in range(z_size)]

    def in_plane(rows, count):
        rows = rows.reshape(plane, count * capacity, model_width)
        rows = lax.all_to_all(rows, ("x", "y"), split_axis=0, concat_axis=0, tiled=True)
        return rows.reshape(plane, count, capacity, model_width)

    def flat(rows):
        return rows.reshape(-1, model_width)

    offsets = [*NEAR, *(d for d in range(2, z_size - 1))]
    near_count, far_count = len(NEAR), z_size - len(NEAR)
    order = jnp.stack([my_z + d for d in offsets]) % z_size

    table = slot_table(routes, gate_probs, sizes, capacity).reshape(z_size, -1)
    table = jnp.pad(table, ((0, 0), (0, model_width - table.shape[1])))
    block = jnp.concatenate([tokens, table], axis=0)
    blocks = lax.all_gather(block, "z", axis=0, tiled=False)
    near_blocks = [block, lax.ppermute(block, "z", up_ring), lax.ppermute(block, "z", down_ring)]

    swap = [(0, 1), (1, 0)]
    weights = [gate_w[0], up_w[0]]
    weights = [v for w in weights for v in (w, lax.ppermute(w, "dp", swap))]
    w_down = jnp.concatenate([down_w[0], lax.ppermute(down_w[0], "dp", swap)], axis=0)

    weights, w_down, near_blocks, order = lax.optimization_barrier(
        (weights, w_down, near_blocks, order)
    )
    near = flat(in_plane(pack_near(order, near_blocks, tok_count, plane, capacity), near_count))
    after = near[:8, :128] + 1
    far = pack_far(order, blocks, after, tok_count, plane, capacity)
    far = flat(in_plane(far, far_count))
    hidden_near, hidden_far = hidden_of(near, far, weights)

    answers = dot(hidden_far, w_down).astype(jnp.bfloat16)
    answers = in_plane(answers, far_count)
    partial = mix_far(order, blocks, answers, tok_count)
    partial, hidden_near = lax.optimization_barrier((partial, hidden_near))
    total = lax.psum_scatter(partial, "z", scatter_dimension=0, tiled=True)[0]

    answers = dot(hidden_near, w_down).astype(jnp.bfloat16)
    answers = in_plane(answers, near_count)
    own, under, over = mix_near(order, near_blocks, answers, tok_count)
    under, over = lax.ppermute(under, "z", down_ring), lax.ppermute(over, "z", up_ring)
    total = total.astype(jnp.float32) + own + under.astype(jnp.float32) + over.astype(jnp.float32)
    return total.astype(jnp.bfloat16)


def solution(mesh):
    experts, dp = mesh.shape["expert"], mesh.shape["dp"]
    x_size = y_size = 4
    z_size = experts // (x_size * y_size)
    grid = Mesh(mesh.devices.reshape(x_size, z_size, y_size, dp), ("x", "z", "y", "dp"))
    every, owner = ("x", "z", "y", "dp"), ("x", "z", "y")
    return jax.shard_map(
        body,
        mesh=grid,
        in_specs=(
            P(every, None),
            P(every, None),
            P(every, None),
            P(owner, None, "dp"),
            P(owner, None, "dp"),
            P(owner, "dp", None),
        ),
        out_specs=P(every, None),
        check_vma=False,
    )
```

```python
import functools

import jax
import jax.numpy as jnp
import numpy as np
from jax import lax
from jax.experimental import pallas as pl
from jax.experimental.pallas import tpu as pltpu
from jax.sharding import Mesh
from jax.sharding import PartitionSpec as P

DEPTH = 512
STEP = 1024
LISTS = 512
NEAR = (0, -1, 1)


def slot_table(routes, gate_probs, sizes, capacity):
    x_size, z_size, y_size = sizes
    tok_count, top_count = routes.shape
    flat = routes.T.reshape(-1)
    token = jnp.arange(tok_count * top_count, dtype=jnp.int32) % tok_count
    earlier = (flat[:, None] == flat[None, :]) & (token[None, :] < token[:, None])
    slot = jnp.sum(earlier.astype(jnp.int32), axis=1)
    ex, ez, ey = flat // (z_size * y_size), flat // y_size % z_size, flat % y_size
    target = ((ez * x_size + ex) * y_size + ey) * capacity + slot
    slots = jnp.arange(x_size * z_size * y_size * capacity, dtype=jnp.int32)
    here = target[None, :] == slots[:, None]
    held = jnp.sum(jnp.where(here, (token + 1).astype(jnp.float32)[None, :], 0.0), axis=1)
    prob = jnp.sum(jnp.where(here, gate_probs.T.reshape(-1)[None, :], 0.0), axis=1)
    high = lax.reduce_precision(prob, 8, 7)
    table = jnp.stack([held, high, prob - high]).reshape(3, z_size, -1)
    return table.transpose(1, 0, 2).astype(jnp.bfloat16)


def hits(row_token, tok_count):
    tokens = lax.broadcasted_iota(jnp.int32, (tok_count, row_token.shape[1]), 0)
    return tokens == row_token.astype(jnp.int32) - 1


def place_rows(here, block):
    place = jnp.where(here, 1.0, 0.0).astype(jnp.bfloat16)
    rows = lax.dot_general(
        place, block, (((0,), (0,)), ((), ())), preferred_element_type=jnp.float32
    )
    return rows.astype(jnp.bfloat16)


def lists_of(rows, me, lanes):
    rows = rows[:, : 3 * lanes].astype(jnp.float32)
    mine = lax.broadcasted_iota(jnp.int32, rows.shape, 0) == me
    rows = jnp.sum(jnp.where(mine, rows, 0.0), axis=0, keepdims=True)
    return [rows[:, r * lanes : (r + 1) * lanes] for r in range(3)]


def mixed(lists, rows, tok_count):
    here = hits(lists[0], tok_count)
    both = jnp.concatenate([jnp.where(here, part, 0.0) for part in lists[1:]], axis=0)
    sums = jnp.dot(both.astype(jnp.bfloat16), rows, preferred_element_type=jnp.float32)
    return sums[:tok_count] + sums[tok_count:]


def pack_near_kernel(order_ref, *refs):
    *list_refs, out_ref = refs
    count = len(list_refs) // 2
    plane, _, capacity, width = out_ref.shape
    for i in range(count):
        token_ref = list_refs[count + i]
        lists = lists_of(list_refs[i][...], order_ref[0], plane * capacity)
        rows = place_rows(hits(lists[0], token_ref.shape[0]), token_ref[...])
        out_ref[:, i] = rows.reshape(plane, capacity, width)


def pack_near(order, blocks, tok_count, plane, capacity):
    count, width = len(blocks), blocks[0].shape[1]
    z_size = blocks[0].shape[0] - tok_count
    below = pl.BlockSpec((z_size, LISTS), lambda i, order: (tok_count // z_size, 0))
    return pl.pallas_call(
        pack_near_kernel,
        grid_spec=pltpu.PrefetchScalarGridSpec(
            num_scalar_prefetch=1,
            grid=(width // STEP,),
            in_specs=[below] * count
            + [pl.BlockSpec((tok_count, STEP), lambda i, order: (0, i))] * count,
            out_specs=pl.BlockSpec((plane, count, capacity, STEP), lambda i, order: (0, 0, 0, i)),
        ),
        out_shape=jax.ShapeDtypeStruct((plane, count, capacity, width), jnp.bfloat16),
        name="pack_near",
    )(order, *blocks, *blocks)


def pack_far_kernel(order_ref, lists_ref, tok_ref, _, out_ref):
    plane, count, capacity, width = out_ref.shape
    for i in range(count):
        src = order_ref[len(NEAR) + i]
        lists = lists_of(lists_ref[src], order_ref[0], plane * capacity)
        rows = place_rows(hits(lists[0], tok_ref.shape[1]), tok_ref[src])
        out_ref[:, i] = rows.reshape(plane, capacity, width)


def pack_far(order, blocks, after, tok_count, plane, capacity):
    z_size, _, width = blocks.shape
    count = z_size - len(NEAR)
    return pl.pallas_call(
        pack_far_kernel,
        grid_spec=pltpu.PrefetchScalarGridSpec(
            num_scalar_prefetch=1,
            grid=(width // STEP,),
            in_specs=[
                pl.BlockSpec((z_size, z_size, LISTS), lambda i, order: (0, tok_count // z_size, 0)),
                pl.BlockSpec((z_size, tok_count, STEP), lambda i, order: (0, 0, i)),
                pl.BlockSpec(after.shape, lambda i, order: (0, 0)),
            ],
            out_specs=pl.BlockSpec((plane, count, capacity, STEP), lambda i, order: (0, 0, 0, i)),
        ),
        out_shape=jax.ShapeDtypeStruct((plane, count, capacity, width), jnp.bfloat16),
        name="pack_far",
    )(order, blocks, blocks, after)


def mix_far_kernel(order_ref, lists_ref, rows_ref, out_ref):
    plane, count, capacity, width = rows_ref.shape
    for i in range(len(NEAR)):
        out_ref[order_ref[i]] = jnp.zeros(out_ref.shape[1:], out_ref.dtype)
    for i in range(count):
        src = order_ref[len(NEAR) + i]
        lists = lists_of(lists_ref[src], order_ref[0], plane * capacity)
        rows = rows_ref[:, i].reshape(plane * capacity, width)
        out_ref[src] = mixed(lists, rows, out_ref.shape[1]).astype(out_ref.dtype)


def mix_far(order, blocks, rows, tok_count):
    plane, count, capacity, width = rows.shape
    z_size = blocks.shape[0]
    return pl.pallas_call(
        mix_far_kernel,
        grid_spec=pltpu.PrefetchScalarGridSpec(
            num_scalar_prefetch=1,
            grid=(width // STEP,),
            in_specs=[
                pl.BlockSpec((z_size, z_size, LISTS), lambda i, order: (0, tok_count // z_size, 0)),
                pl.BlockSpec((plane, count, capacity, STEP), lambda i, order: (0, 0, 0, i)),
            ],
            out_specs=pl.BlockSpec((z_size, tok_count, STEP), lambda i, order: (0, 0, i)),
        ),
        out_shape=jax.ShapeDtypeStruct((z_size, tok_count, width), jnp.bfloat16),
        name="mix_far",
    )(order, blocks, rows)


def mix_near_kernel(order_ref, *refs):
    count = len(refs) // 2
    rows_ref, outs = refs[count], refs[count + 1 :]
    plane, _, capacity, width = rows_ref.shape
    for i in range(count):
        lists = lists_of(refs[i][...], order_ref[0], plane * capacity)
        rows = rows_ref[:, i].reshape(plane * capacity, width)
        outs[i][...] = mixed(lists, rows, outs[i].shape[0]).astype(outs[i].dtype)


def mix_near(order, blocks, rows, tok_count, kind):
    plane, count, capacity, width = rows.shape
    z_size = blocks[0].shape[0] - tok_count
    return pl.pallas_call(
        mix_near_kernel,
        grid_spec=pltpu.PrefetchScalarGridSpec(
            num_scalar_prefetch=1,
            grid=(width // STEP,),
            in_specs=[pl.BlockSpec((z_size, LISTS), lambda i, order: (tok_count // z_size, 0))]
            * count
            + [pl.BlockSpec((plane, count, capacity, STEP), lambda i, order: (0, 0, 0, i))],
            out_specs=[pl.BlockSpec((tok_count, STEP), lambda i, order: (0, i))] * count,
        ),
        out_shape=[jax.ShapeDtypeStruct((tok_count, width), kind)] * count,
        name="mix_near",
    )(order, *blocks, rows)


def hidden_kernel(own_ref, next_ref, far_ref, *refs):
    *weights, out_near, out_far, gate_acc, up_acc = refs
    step, steps = pl.program_id(0), pl.num_programs(0)
    gate, gate_other, up, up_other = (ref[...] for ref in weights)
    gate = jnp.concatenate([gate, gate_other], axis=1)
    up = jnp.concatenate([up, up_other], axis=1)
    rows = jnp.concatenate([own_ref[...], next_ref[...], far_ref[...]], axis=0)

    @pl.when(step == 0)
    def _():
        gate_acc[...] = dot(rows, gate)
        up_acc[...] = dot(rows, up)

    @pl.when((step > 0) & (step < steps - 1))
    def _():
        gate_acc[...] += dot(rows, gate)
        up_acc[...] += dot(rows, up)

    @pl.when(step == steps - 1)
    def _():
        gate_act = gate_acc[...] + dot(rows, gate)
        up_act = up_acc[...] + dot(rows, up)
        hidden = (jax.nn.silu(gate_act) * up_act).astype(out_far.dtype)
        near = out_near.shape[0]
        out_near[...] = hidden[:near]
        out_far[...] = hidden[near:]


def hidden_of(own, beside, far, weights):
    depth, units = weights[0].shape
    groups = [r.shape[0] for r in (own, beside, far)]
    counts = [groups[0] + groups[1], groups[2]]
    return pl.pallas_call(
        hidden_kernel,
        grid=(depth // DEPTH,),
        in_specs=[pl.BlockSpec((c, DEPTH), lambda i: (0, i)) for c in groups]
        + [pl.BlockSpec((DEPTH, units), lambda i: (i, 0))] * 4,
        out_specs=[pl.BlockSpec((c, 2 * units), lambda i: (0, 0)) for c in counts],
        out_shape=[jax.ShapeDtypeStruct((c, 2 * units), jnp.bfloat16) for c in counts],
        scratch_shapes=[pltpu.VMEM((sum(counts), 2 * units), jnp.float32)] * 2,
        compiler_params=pltpu.CompilerParams(vmem_limit_bytes=56 << 20),
        name="hidden",
    )(own, beside, far, *weights)


def dot(a, b):
    return jnp.dot(a, b, preferred_element_type=jnp.float32)


def body(tokens, routes, gate_probs, gate_w, up_w, down_w):
    sizes = tuple(lax.axis_size(a) for a in ("x", "z", "y"))
    x_size, z_size, y_size = sizes
    plane = x_size * y_size
    tok_count, model_width = tokens.shape
    capacity = 2 * tok_count * routes.shape[1] // (plane * z_size)
    my_z = lax.axis_index("z")
    up_ring = [(i, (i + 1) % z_size) for i in range(z_size)]
    down_ring = [(i, (i - 1) % z_size) for i in range(z_size)]

    def in_plane(rows, count):
        rows = rows.reshape(plane, count * capacity, model_width)
        rows = lax.all_to_all(rows, ("x", "y"), split_axis=0, concat_axis=0, tiled=True)
        return rows.reshape(plane, count, capacity, model_width)

    def flat(rows):
        return rows.reshape(-1, model_width)

    offsets = [*NEAR, *(d for d in range(2, z_size - 1))]
    far_count = z_size - len(NEAR)
    order = jnp.stack([my_z + d for d in offsets]) % z_size

    table = slot_table(routes, gate_probs, sizes, capacity).reshape(z_size, -1)
    table = jnp.pad(table, ((0, 0), (0, model_width - table.shape[1])))
    block = jnp.concatenate([tokens, table], axis=0)
    blocks = lax.all_gather(block, "z", axis=0, tiled=False)
    own_blocks = [block]
    next_blocks = [lax.ppermute(block, "z", up_ring), lax.ppermute(block, "z", down_ring)]

    swap = [(0, 1), (1, 0)]
    weights = [gate_w[0], up_w[0]]
    weights = [v for w in weights for v in (w, lax.ppermute(w, "dp", swap))]
    down_other = lax.ppermute(down_w[0], "dp", swap)

    def packed(blocks):
        return pack_near(order, blocks, tok_count, plane, capacity)

    own = flat(in_plane(packed(own_blocks), len(own_blocks)))
    after = own[:8, :128] + 1
    next_blocks, weights, down_other, order, after = lax.optimization_barrier(
        (next_blocks, weights, down_other, order, after)
    )
    beside = flat(in_plane(packed(next_blocks), len(next_blocks)))
    after, down_other = lax.optimization_barrier((after + beside[:8, :128], down_other))
    w_down = jnp.concatenate([down_w[0], down_other], axis=0)
    after, w_down = lax.optimization_barrier((after, w_down))
    far = pack_far(order, blocks, after, tok_count, plane, capacity)
    far = flat(in_plane(far, far_count))
    hidden_near, hidden_far = hidden_of(own, beside, far, weights)

    answers = dot(hidden_far, w_down).astype(jnp.bfloat16)
    answers = in_plane(answers, far_count)
    partial = mix_far(order, blocks, answers, tok_count)
    partial, hidden_near = lax.optimization_barrier((partial, hidden_near))
    total = lax.psum_scatter(partial, "z", scatter_dimension=0, tiled=True)[0]

    answers = dot(hidden_near, w_down).astype(jnp.bfloat16)
    split = own.shape[0]
    answers_own, answers = answers[:split], answers[split:]
    answers, answers_own = lax.optimization_barrier((answers, answers_own))
    answers = in_plane(answers, len(next_blocks))
    under, over = mix_near(order, next_blocks, answers, tok_count, jnp.bfloat16)
    under, over, answers_own = lax.optimization_barrier((under, over, answers_own))
    under, over = lax.ppermute(under, "z", down_ring), lax.ppermute(over, "z", up_ring)
    answers_own = in_plane(answers_own, len(own_blocks))
    (mine,) = mix_near(order, own_blocks, answers_own, tok_count, jnp.float32)
    total = total.astype(jnp.float32) + mine + under.astype(jnp.float32) + over.astype(jnp.float32)
    return total.astype(jnp.bfloat16)


def solution(mesh):
    experts, dp = mesh.shape["expert"], mesh.shape["dp"]
    x_size = y_size = 4
    z_size = experts // (x_size * y_size)
    grid = Mesh(mesh.devices.reshape(x_size, z_size, y_size, dp), ("x", "z", "y", "dp"))
    every, owner = ("x", "z", "y", "dp"), ("x", "z", "y")
    return jax.shard_map(
        body,
        mesh=grid,
        in_specs=(
            P(every, None),
            P(every, None),
            P(every, None),
            P(owner, None, "dp"),
            P(owner, None, "dp"),
            P(owner, "dp", None),
        ),
        out_specs=P(every, None),
        check_vma=False,
    )
```

```python
import functools

import jax
import jax.numpy as jnp
import numpy as np
from jax import lax
from jax.experimental import pallas as pl
from jax.experimental.pallas import tpu as pltpu
from jax.sharding import Mesh
from jax.sharding import PartitionSpec as P

DEPTH = 512
STEP = 1024
LISTS = 512
NEAR = (0,)
ARRIVE = (2048, 2048)
LEAVE = (2048, 2048)


def slot_table(routes, gate_probs, sizes, capacity):
    x_size, z_size, y_size = sizes
    tok_count, top_count = routes.shape
    flat = routes.T.reshape(-1)
    token = jnp.arange(tok_count * top_count, dtype=jnp.int32) % tok_count
    earlier = (flat[:, None] == flat[None, :]) & (token[None, :] < token[:, None])
    slot = jnp.sum(earlier.astype(jnp.int32), axis=1)
    ex, ez, ey = flat // (z_size * y_size), flat // y_size % z_size, flat % y_size
    target = ((ez * x_size + ex) * y_size + ey) * capacity + slot
    slots = jnp.arange(x_size * z_size * y_size * capacity, dtype=jnp.int32)
    here = target[None, :] == slots[:, None]
    held = jnp.sum(jnp.where(here, (token + 1).astype(jnp.float32)[None, :], 0.0), axis=1)
    prob = jnp.sum(jnp.where(here, gate_probs.T.reshape(-1)[None, :], 0.0), axis=1)
    high = lax.reduce_precision(prob, 8, 7)
    table = jnp.stack([held, high, prob - high]).reshape(3, z_size, -1)
    return table.transpose(1, 0, 2).astype(jnp.bfloat16)


def hits(row_token, tok_count):
    tokens = lax.broadcasted_iota(jnp.int32, (tok_count, row_token.shape[1]), 0)
    return tokens == row_token.astype(jnp.int32) - 1


def place_rows(here, block):
    place = jnp.where(here, 1.0, 0.0).astype(jnp.bfloat16)
    rows = lax.dot_general(
        place, block, (((0,), (0,)), ((), ())), preferred_element_type=jnp.float32
    )
    return rows.astype(jnp.bfloat16)


def lists_of(rows, me, lanes):
    rows = rows[:, : 3 * lanes].astype(jnp.float32)
    mine = lax.broadcasted_iota(jnp.int32, rows.shape, 0) == me
    rows = jnp.sum(jnp.where(mine, rows, 0.0), axis=0, keepdims=True)
    return [rows[:, r * lanes : (r + 1) * lanes] for r in range(3)]


def mixed(lists, rows, tok_count):
    here = hits(lists[0], tok_count)
    both = jnp.concatenate([jnp.where(here, part, 0.0) for part in lists[1:]], axis=0)
    sums = jnp.dot(both.astype(jnp.bfloat16), rows, preferred_element_type=jnp.float32)
    return sums[:tok_count] + sums[tok_count:]


def pack_near_kernel(order_ref, *refs):
    *list_refs, out_ref = refs
    count = len(list_refs) // 2
    plane, _, capacity, width = out_ref.shape
    for i in range(count):
        token_ref = list_refs[count + i]
        lists = lists_of(list_refs[i][...], order_ref[0], plane * capacity)
        rows = place_rows(hits(lists[0], token_ref.shape[0]), token_ref[...])
        out_ref[:, i] = rows.reshape(plane, capacity, width)


def pack_near(order, blocks, tok_count, plane, capacity):
    count, width = len(blocks), blocks[0].shape[1]
    z_size = blocks[0].shape[0] - tok_count
    below = pl.BlockSpec((z_size, LISTS), lambda i, order: (tok_count // z_size, 0))
    return pl.pallas_call(
        pack_near_kernel,
        grid_spec=pltpu.PrefetchScalarGridSpec(
            num_scalar_prefetch=1,
            grid=(width // STEP,),
            in_specs=[below] * count
            + [pl.BlockSpec((tok_count, STEP), lambda i, order: (0, i))] * count,
            out_specs=pl.BlockSpec((plane, count, capacity, STEP), lambda i, order: (0, 0, 0, i)),
        ),
        out_shape=jax.ShapeDtypeStruct((plane, count, capacity, width), jnp.bfloat16),
        name="pack_near",
    )(order, *blocks, *blocks)


def pack_far_kernel(order_ref, lists_ref, tok_ref, _, out_ref):
    plane, count, capacity, width = out_ref.shape
    for i in range(count):
        src = order_ref[len(NEAR) + i]
        lists = lists_of(lists_ref[src], order_ref[0], plane * capacity)
        rows = place_rows(hits(lists[0], tok_ref.shape[1]), tok_ref[src])
        out_ref[:, i] = rows.reshape(plane, capacity, width)


def pack_far(order, listed, blocks, after, tok_count, plane, capacity):
    z_size, _, width = blocks.shape
    count = z_size - len(NEAR)
    return pl.pallas_call(
        pack_far_kernel,
        grid_spec=pltpu.PrefetchScalarGridSpec(
            num_scalar_prefetch=1,
            grid=(width // STEP,),
            in_specs=[
                pl.BlockSpec((z_size, z_size, LISTS), lambda i, order: (0, tok_count // z_size, 0)),
                pl.BlockSpec((z_size, tok_count, STEP), lambda i, order: (0, 0, i)),
                pl.BlockSpec(after.shape, lambda i, order: (0, 0)),
            ],
            out_specs=pl.BlockSpec((plane, count, capacity, STEP), lambda i, order: (0, 0, 0, i)),
        ),
        out_shape=jax.ShapeDtypeStruct((plane, count, capacity, width), jnp.bfloat16),
        name="pack_far",
    )(order, listed, blocks, after)


def mix_far_kernel(order_ref, lists_ref, rows_ref, out_ref):
    plane, count, capacity, width = rows_ref.shape
    for i in range(len(NEAR)):
        out_ref[order_ref[i]] = jnp.zeros(out_ref.shape[1:], out_ref.dtype)
    for i in range(count):
        src = order_ref[len(NEAR) + i]
        lists = lists_of(lists_ref[src], order_ref[0], plane * capacity)
        rows = rows_ref[:, i].reshape(plane * capacity, width)
        out_ref[src] = mixed(lists, rows, out_ref.shape[1]).astype(out_ref.dtype)


def mix_far(order, listed, rows, tok_count):
    plane, count, capacity, width = rows.shape
    z_size = listed.shape[0]
    return pl.pallas_call(
        mix_far_kernel,
        grid_spec=pltpu.PrefetchScalarGridSpec(
            num_scalar_prefetch=1,
            grid=(width // STEP,),
            in_specs=[
                pl.BlockSpec((z_size, z_size, LISTS), lambda i, order: (0, tok_count // z_size, 0)),
                pl.BlockSpec((plane, count, capacity, STEP), lambda i, order: (0, 0, 0, i)),
            ],
            out_specs=pl.BlockSpec((z_size, tok_count, STEP), lambda i, order: (0, 0, i)),
        ),
        out_shape=jax.ShapeDtypeStruct((z_size, tok_count, width), jnp.bfloat16),
        name="mix_far",
    )(order, listed, rows)


def mix_near_kernel(order_ref, *refs):
    count = len(NEAR)
    rows_ref, outs = refs[count], refs[count + 1 :]
    plane, _, capacity, width = rows_ref.shape
    for i in range(count):
        lists = lists_of(refs[i][...], order_ref[0], plane * capacity)
        rows = rows_ref[:, i].reshape(plane * capacity, width)
        outs[i][...] = mixed(lists, rows, outs[i].shape[0]).astype(outs[i].dtype)


def mix_near(order, blocks, rows, tok_count):
    plane, count, capacity, width = rows.shape
    z_size = blocks[0].shape[0] - tok_count
    kinds = [jnp.bfloat16 if offset else jnp.float32 for offset in NEAR]
    return pl.pallas_call(
        mix_near_kernel,
        grid_spec=pltpu.PrefetchScalarGridSpec(
            num_scalar_prefetch=1,
            grid=(width // STEP,),
            in_specs=[pl.BlockSpec((z_size, LISTS), lambda i, order: (tok_count // z_size, 0))]
            * count
            + [pl.BlockSpec((plane, count, capacity, STEP), lambda i, order: (0, 0, 0, i))],
            out_specs=[pl.BlockSpec((tok_count, STEP), lambda i, order: (0, i))] * count,
        ),
        out_shape=[jax.ShapeDtypeStruct((tok_count, width), kind) for kind in kinds],
        name="mix_near",
    )(order, *blocks, rows)


def hidden_kernel(own_ref, first_ref, second_ref, *refs, split):
    *weights, out_own, out_far, gate_acc, up_acc = refs
    step, steps = pl.program_id(0), pl.num_programs(0)

    def products(far_ref):
        gate, gate_other, up, up_other = (ref[...] for ref in weights)
        gate = jnp.concatenate([gate, gate_other], axis=1)
        up = jnp.concatenate([up, up_other], axis=1)
        rows = jnp.concatenate([own_ref[...], far_ref[...]], axis=0)
        return dot(rows, gate), dot(rows, up)

    @pl.when(step == 0)
    def _():
        gate_acc[...], up_acc[...] = products(first_ref)

    @pl.when((step > 0) & (step < split))
    def _():
        gate, up = products(first_ref)
        gate_acc[...] += gate
        up_acc[...] += up

    @pl.when((step >= split) & (step < steps - 1))
    def _():
        gate, up = products(second_ref)
        gate_acc[...] += gate
        up_acc[...] += up

    @pl.when(step == steps - 1)
    def _():
        gate, up = products(second_ref)
        hidden = jax.nn.silu(gate_acc[...] + gate) * (up_acc[...] + up)
        count = out_own.shape[0]
        out_own[...] = hidden[:count].astype(out_own.dtype)
        out_far[...] = hidden[count:].astype(out_far.dtype)


def hidden_of(own, first, second, weights):
    depth, units = weights[0].shape
    counts = [own.shape[0], first.shape[0]]
    split = first.shape[1] // DEPTH
    return pl.pallas_call(
        functools.partial(hidden_kernel, split=split),
        grid=(depth // DEPTH,),
        in_specs=[
            pl.BlockSpec((counts[0], DEPTH), lambda i: (0, i)),
            pl.BlockSpec((counts[1], DEPTH), lambda i: (0, jnp.minimum(i, split - 1))),
            pl.BlockSpec((counts[1], DEPTH), lambda i: (0, jnp.maximum(i - split, 0))),
        ]
        + [pl.BlockSpec((DEPTH, units), lambda i: (i, 0))] * 4,
        out_specs=[pl.BlockSpec((c, 2 * units), lambda i: (0, 0)) for c in counts],
        out_shape=[jax.ShapeDtypeStruct((c, 2 * units), jnp.bfloat16) for c in counts],
        scratch_shapes=[pltpu.VMEM((sum(counts), 2 * units), jnp.float32)] * 2,
        compiler_params=pltpu.CompilerParams(vmem_limit_bytes=56 << 20),
        name="hidden",
    )(own, first, second, *weights)


def cuts(widths):
    ends = np.cumsum(widths)
    return [slice(int(end) - width, int(end)) for width, end in zip(widths, ends, strict=True)]


def dot(a, b):
    return jnp.dot(a, b, preferred_element_type=jnp.float32)


def body(tokens, routes, gate_probs, gate_w, up_w, down_w):
    sizes = tuple(lax.axis_size(a) for a in ("x", "z", "y"))
    x_size, z_size, y_size = sizes
    plane = x_size * y_size
    tok_count, model_width = tokens.shape
    capacity = 2 * tok_count * routes.shape[1] // (plane * z_size)
    my_z = lax.axis_index("z")

    def in_plane(rows, count):
        width = rows.shape[-1]
        rows = rows.reshape(plane, count * capacity, width)
        rows = lax.all_to_all(rows, ("x", "y"), split_axis=0, concat_axis=0, tiled=True)
        return rows.reshape(plane, count, capacity, width)

    def flat(rows):
        return rows.reshape(-1, rows.shape[-1])

    own_count, far_count = len(NEAR), z_size - len(NEAR)
    order = jnp.stack([my_z + d for d in range(z_size)]) % z_size
    into, back = cuts(ARRIVE), cuts(LEAVE)

    table = slot_table(routes, gate_probs, sizes, capacity).reshape(z_size, -1)
    table = jnp.pad(table, ((0, 0), (0, ARRIVE[0] - table.shape[1])))
    top = jnp.concatenate([tokens[:, into[0]], table], axis=0)
    first = lax.all_gather(top, "z", axis=0, tiled=False)
    second = lax.all_gather(tokens[:, into[1]], "z", axis=0, tiled=False)
    mine = jnp.pad(table, ((0, 0), (0, ARRIVE[1])))
    mine = [jnp.concatenate([tokens, mine], axis=0)]

    swap = [(0, 1), (1, 0)]
    weights = [gate_w[0], up_w[0]]
    weights = [v for w in weights for v in (w, lax.ppermute(w, "dp", swap))]
    down_other = lax.ppermute(down_w[0], "dp", swap)

    own = flat(in_plane(pack_near(order, mine, tok_count, plane, capacity), own_count))
    after, weights, down_other = lax.optimization_barrier(
        (own[:8, :128] + 1, weights, down_other)
    )
    w_down = jnp.concatenate([down_w[0], down_other], axis=0)
    after, w_down = lax.optimization_barrier((after, w_down))
    far = []
    for block in (first, second):
        rows = pack_far(order, first, block, after, tok_count, plane, capacity)
        far.append(flat(in_plane(rows, far_count)))
        after = far[-1][:8, :128] + 1
    hidden_own, hidden_far = hidden_of(own, *far, weights)

    totals = []
    for part in back:
        answers = dot(hidden_far, w_down[:, part]).astype(jnp.bfloat16)
        partial = mix_far(order, first, in_plane(answers, far_count), tok_count)
        partial, hidden_far, hidden_own = lax.optimization_barrier(
            (partial, hidden_far, hidden_own)
        )
        totals.append(lax.psum_scatter(partial, "z", scatter_dimension=0, tiled=True)[0])

    answers = dot(hidden_own, w_down).astype(jnp.bfloat16)
    (mine,) = mix_near(order, mine, in_plane(answers, own_count), tok_count)
    total = jnp.concatenate(totals, axis=1).astype(jnp.float32) + mine
    return total.astype(jnp.bfloat16)


def solution(mesh):
    experts, dp = mesh.shape["expert"], mesh.shape["dp"]
    x_size = y_size = 4
    z_size = experts // (x_size * y_size)
    grid = Mesh(mesh.devices.reshape(x_size, z_size, y_size, dp), ("x", "z", "y", "dp"))
    every, owner = ("x", "z", "y", "dp"), ("x", "z", "y")
    return jax.shard_map(
        body,
        mesh=grid,
        in_specs=(
            P(every, None),
            P(every, None),
            P(every, None),
            P(owner, None, "dp"),
            P(owner, None, "dp"),
            P(owner, "dp", None),
        ),
        out_specs=P(every, None),
        check_vma=False,
    )
```

```python
import functools

import jax
import jax.numpy as jnp
import numpy as np
from jax import lax
from jax.experimental import pallas as pl
from jax.experimental.pallas import tpu as pltpu
from jax.sharding import Mesh
from jax.sharding import PartitionSpec as P

DEPTH = 512
STEP = 1024
LISTS = 512
NEAR = (0, 1)


def slot_table(routes, gate_probs, sizes, capacity):
    x_size, z_size, y_size = sizes
    tok_count, top_count = routes.shape
    flat = routes.T.reshape(-1)
    token = jnp.arange(tok_count * top_count, dtype=jnp.int32) % tok_count
    earlier = (flat[:, None] == flat[None, :]) & (token[None, :] < token[:, None])
    slot = jnp.sum(earlier.astype(jnp.int32), axis=1)
    ex, ez, ey = flat // (z_size * y_size), flat // y_size % z_size, flat % y_size
    target = ((ez * x_size + ex) * y_size + ey) * capacity + slot
    slots = jnp.arange(x_size * z_size * y_size * capacity, dtype=jnp.int32)
    here = target[None, :] == slots[:, None]
    held = jnp.sum(jnp.where(here, (token + 1).astype(jnp.float32)[None, :], 0.0), axis=1)
    prob = jnp.sum(jnp.where(here, gate_probs.T.reshape(-1)[None, :], 0.0), axis=1)
    high = lax.reduce_precision(prob, 8, 7)
    table = jnp.stack([held, high, prob - high]).reshape(3, z_size, -1)
    return table.transpose(1, 0, 2).astype(jnp.bfloat16)


def hits(row_token, tok_count):
    tokens = lax.broadcasted_iota(jnp.int32, (tok_count, row_token.shape[1]), 0)
    return tokens == row_token.astype(jnp.int32) - 1


def place_rows(here, block):
    place = jnp.where(here, 1.0, 0.0).astype(jnp.bfloat16)
    rows = lax.dot_general(
        place, block, (((0,), (0,)), ((), ())), preferred_element_type=jnp.float32
    )
    return rows.astype(jnp.bfloat16)


def lists_of(rows, me, lanes):
    rows = rows[:, : 3 * lanes].astype(jnp.float32)
    mine = lax.broadcasted_iota(jnp.int32, rows.shape, 0) == me
    rows = jnp.sum(jnp.where(mine, rows, 0.0), axis=0, keepdims=True)
    return [rows[:, r * lanes : (r + 1) * lanes] for r in range(3)]


def mixed(lists, rows, tok_count):
    here = hits(lists[0], tok_count)
    both = jnp.concatenate([jnp.where(here, part, 0.0) for part in lists[1:]], axis=0)
    sums = jnp.dot(both.astype(jnp.bfloat16), rows, preferred_element_type=jnp.float32)
    return sums[:tok_count] + sums[tok_count:]


def pack_near_kernel(order_ref, *refs):
    *list_refs, out_ref = refs
    count = len(list_refs) // 2
    plane, _, capacity, width = out_ref.shape
    for i in range(count):
        token_ref = list_refs[count + i]
        lists = lists_of(list_refs[i][...], order_ref[0], plane * capacity)
        rows = place_rows(hits(lists[0], token_ref.shape[0]), token_ref[...])
        out_ref[:, i] = rows.reshape(plane, capacity, width)


def pack_near(order, blocks, tok_count, plane, capacity):
    count, width = len(blocks), blocks[0].shape[1]
    z_size = blocks[0].shape[0] - tok_count
    below = pl.BlockSpec((z_size, LISTS), lambda i, order: (tok_count // z_size, 0))
    return pl.pallas_call(
        pack_near_kernel,
        grid_spec=pltpu.PrefetchScalarGridSpec(
            num_scalar_prefetch=1,
            grid=(width // STEP,),
            in_specs=[below] * count
            + [pl.BlockSpec((tok_count, STEP), lambda i, order: (0, i))] * count,
            out_specs=pl.BlockSpec((plane, count, capacity, STEP), lambda i, order: (0, 0, 0, i)),
        ),
        out_shape=jax.ShapeDtypeStruct((plane, count, capacity, width), jnp.bfloat16),
        name="pack_near",
    )(order, *blocks, *blocks)


def pack_far_kernel(order_ref, lists_ref, tok_ref, _, out_ref):
    plane, count, capacity, width = out_ref.shape
    for i in range(count):
        src = order_ref[len(NEAR) + i]
        lists = lists_of(lists_ref[src], order_ref[0], plane * capacity)
        rows = place_rows(hits(lists[0], tok_ref.shape[1]), tok_ref[src])
        out_ref[:, i] = rows.reshape(plane, capacity, width)


def pack_far(order, blocks, after, tok_count, plane, capacity):
    z_size, _, width = blocks.shape
    count = z_size - len(NEAR)
    return pl.pallas_call(
        pack_far_kernel,
        grid_spec=pltpu.PrefetchScalarGridSpec(
            num_scalar_prefetch=1,
            grid=(width // STEP,),
            in_specs=[
                pl.BlockSpec((z_size, z_size, LISTS), lambda i, order: (0, tok_count // z_size, 0)),
                pl.BlockSpec((z_size, tok_count, STEP), lambda i, order: (0, 0, i)),
                pl.BlockSpec(after.shape, lambda i, order: (0, 0)),
            ],
            out_specs=pl.BlockSpec((plane, count, capacity, STEP), lambda i, order: (0, 0, 0, i)),
        ),
        out_shape=jax.ShapeDtypeStruct((plane, count, capacity, width), jnp.bfloat16),
        name="pack_far",
    )(order, blocks, blocks, after)


def mix_far_kernel(order_ref, lists_ref, rows_ref, out_ref):
    plane, count, capacity, width = rows_ref.shape
    for i in range(len(NEAR)):
        out_ref[order_ref[i]] = jnp.zeros(out_ref.shape[1:], out_ref.dtype)
    for i in range(count):
        src = order_ref[len(NEAR) + i]
        lists = lists_of(lists_ref[src], order_ref[0], plane * capacity)
        rows = rows_ref[:, i].reshape(plane * capacity, width)
        out_ref[src] = mixed(lists, rows, out_ref.shape[1]).astype(out_ref.dtype)


def mix_far(order, blocks, rows, tok_count):
    plane, count, capacity, width = rows.shape
    z_size = blocks.shape[0]
    return pl.pallas_call(
        mix_far_kernel,
        grid_spec=pltpu.PrefetchScalarGridSpec(
            num_scalar_prefetch=1,
            grid=(width // STEP,),
            in_specs=[
                pl.BlockSpec((z_size, z_size, LISTS), lambda i, order: (0, tok_count // z_size, 0)),
                pl.BlockSpec((plane, count, capacity, STEP), lambda i, order: (0, 0, 0, i)),
            ],
            out_specs=pl.BlockSpec((z_size, tok_count, STEP), lambda i, order: (0, 0, i)),
        ),
        out_shape=jax.ShapeDtypeStruct((z_size, tok_count, width), jnp.bfloat16),
        name="mix_far",
    )(order, blocks, rows)


def mix_near_kernel(order_ref, *refs):
    count = len(NEAR)
    rows_ref, outs = refs[count], refs[count + 1 :]
    plane, _, capacity, width = rows_ref.shape
    for i in range(count):
        lists = lists_of(refs[i][...], order_ref[0], plane * capacity)
        rows = rows_ref[:, i].reshape(plane * capacity, width)
        outs[i][...] = mixed(lists, rows, outs[i].shape[0]).astype(outs[i].dtype)


def mix_near(order, blocks, rows, tok_count):
    plane, count, capacity, width = rows.shape
    z_size = blocks[0].shape[0] - tok_count
    kinds = [jnp.bfloat16 if offset else jnp.float32 for offset in NEAR]
    return pl.pallas_call(
        mix_near_kernel,
        grid_spec=pltpu.PrefetchScalarGridSpec(
            num_scalar_prefetch=1,
            grid=(width // STEP,),
            in_specs=[pl.BlockSpec((z_size, LISTS), lambda i, order: (tok_count // z_size, 0))]
            * count
            + [pl.BlockSpec((plane, count, capacity, STEP), lambda i, order: (0, 0, 0, i))],
            out_specs=[pl.BlockSpec((tok_count, STEP), lambda i, order: (0, i))] * count,
        ),
        out_shape=[jax.ShapeDtypeStruct((tok_count, width), kind) for kind in kinds],
        name="mix_near",
    )(order, *blocks, rows)


def hidden_kernel(near_ref, far_ref, *refs):
    *weights, out_near, out_far, gate_acc, up_acc = refs
    step, steps = pl.program_id(0), pl.num_programs(0)
    gate, gate_other, up, up_other = (ref[...] for ref in weights)
    gate = jnp.concatenate([gate, gate_other], axis=1)
    up = jnp.concatenate([up, up_other], axis=1)
    rows = jnp.concatenate([near_ref[...], far_ref[...]], axis=0)

    @pl.when(step == 0)
    def _():
        gate_acc[...] = dot(rows, gate)
        up_acc[...] = dot(rows, up)

    @pl.when((step > 0) & (step < steps - 1))
    def _():
        gate_acc[...] += dot(rows, gate)
        up_acc[...] += dot(rows, up)

    @pl.when(step == steps - 1)
    def _():
        hidden = jax.nn.silu(gate_acc[...] + dot(rows, gate)) * (up_acc[...] + dot(rows, up))
        count = out_near.shape[0]
        out_near[...] = hidden[:count].astype(out_near.dtype)
        out_far[...] = hidden[count:].astype(out_far.dtype)


def hidden_of(near, far, weights):
    depth, units = weights[0].shape
    counts = [near.shape[0], far.shape[0]]
    return pl.pallas_call(
        hidden_kernel,
        grid=(depth // DEPTH,),
        in_specs=[pl.BlockSpec((c, DEPTH), lambda i: (0, i)) for c in counts]
        + [pl.BlockSpec((DEPTH, units), lambda i: (i, 0))] * 4,
        out_specs=[pl.BlockSpec((c, 2 * units), lambda i: (0, 0)) for c in counts],
        out_shape=[jax.ShapeDtypeStruct((c, 2 * units), jnp.bfloat16) for c in counts],
        scratch_shapes=[pltpu.VMEM((sum(counts), 2 * units), jnp.float32)] * 2,
        compiler_params=pltpu.CompilerParams(vmem_limit_bytes=56 << 20),
        name="hidden",
    )(near, far, *weights)


def dot(a, b):
    return jnp.dot(a, b, preferred_element_type=jnp.float32)


def body(tokens, routes, gate_probs, gate_w, up_w, down_w):
    sizes = tuple(lax.axis_size(a) for a in ("x", "z", "y"))
    x_size, z_size, y_size = sizes
    plane = x_size * y_size
    tok_count, model_width = tokens.shape
    capacity = 2 * tok_count * routes.shape[1] // (plane * z_size)
    my_z = lax.axis_index("z")
    up_ring = [(i, (i + 1) % z_size) for i in range(z_size)]
    down_ring = [(i, (i - 1) % z_size) for i in range(z_size)]

    def in_plane(rows, count):
        rows = rows.reshape(plane, count * capacity, model_width)
        rows = lax.all_to_all(rows, ("x", "y"), split_axis=0, concat_axis=0, tiled=True)
        return rows.reshape(plane, count, capacity, model_width)

    def flat(rows):
        return rows.reshape(-1, model_width)

    offsets = [*NEAR, *range(len(NEAR), z_size)]
    near_count, far_count = len(NEAR), z_size - len(NEAR)
    order = jnp.stack([my_z + d for d in offsets]) % z_size

    table = slot_table(routes, gate_probs, sizes, capacity).reshape(z_size, -1)
    table = jnp.pad(table, ((0, 0), (0, model_width - table.shape[1])))
    block = jnp.concatenate([tokens, table], axis=0)
    blocks = lax.all_gather(block, "z", axis=0, tiled=False)
    near_blocks = [block, lax.ppermute(block, "z", down_ring)]

    swap = [(0, 1), (1, 0)]
    weights = [gate_w[0], up_w[0]]
    weights = [v for w in weights for v in (w, lax.ppermute(w, "dp", swap))]
    w_down = jnp.concatenate([down_w[0], lax.ppermute(down_w[0], "dp", swap)], axis=0)

    weights, w_down, near_blocks, order = lax.optimization_barrier(
        (weights, w_down, near_blocks, order)
    )
    near = flat(in_plane(pack_near(order, near_blocks, tok_count, plane, capacity), near_count))
    after = near[:8, :128] + 1
    far = pack_far(order, blocks, after, tok_count, plane, capacity)
    far = flat(in_plane(far, far_count))
    hidden_near, hidden_far = hidden_of(near, far, weights)

    answers = dot(hidden_far, w_down).astype(jnp.bfloat16)
    answers = in_plane(answers, far_count)
    partial = mix_far(order, blocks, answers, tok_count)
    partial, hidden_near = lax.optimization_barrier((partial, hidden_near))
    total = lax.psum_scatter(partial, "z", scatter_dimension=0, tiled=True)[0]

    answers = dot(hidden_near, w_down).astype(jnp.bfloat16)
    answers = in_plane(answers, near_count)
    own, over = mix_near(order, near_blocks, answers, tok_count)
    over = lax.ppermute(over, "z", up_ring)
    total = total.astype(jnp.float32) + own + over.astype(jnp.float32)
    return total.astype(jnp.bfloat16)


def solution(mesh):
    experts, dp = mesh.shape["expert"], mesh.shape["dp"]
    x_size = y_size = 4
    z_size = experts // (x_size * y_size)
    grid = Mesh(mesh.devices.reshape(x_size, z_size, y_size, dp), ("x", "z", "y", "dp"))
    every, owner = ("x", "z", "y", "dp"), ("x", "z", "y")
    return jax.shard_map(
        body,
        mesh=grid,
        in_specs=(
            P(every, None),
            P(every, None),
            P(every, None),
            P(owner, None, "dp"),
            P(owner, None, "dp"),
            P(owner, "dp", None),
        ),
        out_specs=P(every, None),
        check_vma=False,
    )
```

```python
import functools

import jax
import jax.numpy as jnp
import numpy as np
from jax import lax
from jax.experimental import pallas as pl
from jax.experimental.pallas import tpu as pltpu
from jax.sharding import Mesh
from jax.sharding import PartitionSpec as P

DEPTH = 512
STEP = 2048
LISTS = 512
NEAR = (0, -1, 1)


def slot_table(routes, gate_probs, sizes, capacity):
    x_size, z_size, y_size = sizes
    tok_count, top_count = routes.shape
    flat = routes.T.reshape(-1)
    token = jnp.arange(tok_count * top_count, dtype=jnp.int32) % tok_count
    earlier = (flat[:, None] == flat[None, :]) & (token[None, :] < token[:, None])
    slot = jnp.sum(earlier.astype(jnp.int32), axis=1)
    ex, ez, ey = flat // (z_size * y_size), flat // y_size % z_size, flat % y_size
    target = ((ez * x_size + ex) * y_size + ey) * capacity + slot
    slots = jnp.arange(x_size * z_size * y_size * capacity, dtype=jnp.int32)
    here = target[None, :] == slots[:, None]
    held = jnp.sum(jnp.where(here, (token + 1).astype(jnp.float32)[None, :], 0.0), axis=1)
    prob = jnp.sum(jnp.where(here, gate_probs.T.reshape(-1)[None, :], 0.0), axis=1)
    high = lax.reduce_precision(prob, 8, 7)
    table = jnp.stack([held, high, prob - high]).reshape(3, z_size, -1)
    return table.transpose(1, 0, 2).astype(jnp.bfloat16)


def hits(row_token, tok_count):
    tokens = lax.broadcasted_iota(jnp.int32, (tok_count, row_token.shape[1]), 0)
    return tokens == row_token.astype(jnp.int32) - 1


def place_rows(here, block):
    place = jnp.where(here, 1.0, 0.0).astype(jnp.bfloat16)
    rows = lax.dot_general(
        place, block, (((0,), (0,)), ((), ())), preferred_element_type=jnp.float32
    )
    return rows.astype(jnp.bfloat16)


def lists_of(rows, me, lanes):
    rows = rows[:, : 3 * lanes].astype(jnp.float32)
    mine = lax.broadcasted_iota(jnp.int32, rows.shape, 0) == me
    rows = jnp.sum(jnp.where(mine, rows, 0.0), axis=0, keepdims=True)
    return [rows[:, r * lanes : (r + 1) * lanes] for r in range(3)]


def mixed(lists, rows, tok_count):
    here = hits(lists[0], tok_count)
    both = jnp.concatenate([jnp.where(here, part, 0.0) for part in lists[1:]], axis=0)
    sums = jnp.dot(both.astype(jnp.bfloat16), rows, preferred_element_type=jnp.float32)
    return sums[:tok_count] + sums[tok_count:]


def pack_near_kernel(order_ref, *refs):
    *list_refs, out_ref = refs
    count = len(list_refs) // 2
    plane, _, capacity, width = out_ref.shape
    for i in range(count):
        token_ref = list_refs[count + i]
        lists = lists_of(list_refs[i][...], order_ref[0], plane * capacity)
        rows = place_rows(hits(lists[0], token_ref.shape[0]), token_ref[...])
        out_ref[:, i] = rows.reshape(plane, capacity, width)


def pack_near(order, blocks, tok_count, plane, capacity):
    count, width = len(blocks), blocks[0].shape[1]
    z_size = blocks[0].shape[0] - tok_count
    below = pl.BlockSpec((z_size, LISTS), lambda i, order: (tok_count // z_size, 0))
    return pl.pallas_call(
        pack_near_kernel,
        grid_spec=pltpu.PrefetchScalarGridSpec(
            num_scalar_prefetch=1,
            grid=(width // STEP,),
            in_specs=[below] * count
            + [pl.BlockSpec((tok_count, STEP), lambda i, order: (0, i))] * count,
            out_specs=pl.BlockSpec((plane, count, capacity, STEP), lambda i, order: (0, 0, 0, i)),
        ),
        out_shape=jax.ShapeDtypeStruct((plane, count, capacity, width), jnp.bfloat16),
        name="pack_near",
    )(order, *blocks, *blocks)


def pack_far_kernel(order_ref, lists_ref, tok_ref, _, out_ref):
    plane, count, capacity, width = out_ref.shape
    for i in range(count):
        src = order_ref[len(NEAR) + i]
        lists = lists_of(lists_ref[src], order_ref[0], plane * capacity)
        rows = place_rows(hits(lists[0], tok_ref.shape[1]), tok_ref[src])
        out_ref[:, i] = rows.reshape(plane, capacity, width)


def pack_far(order, blocks, after, tok_count, plane, capacity):
    z_size, _, width = blocks.shape
    count = z_size - len(NEAR)
    return pl.pallas_call(
        pack_far_kernel,
        grid_spec=pltpu.PrefetchScalarGridSpec(
            num_scalar_prefetch=1,
            grid=(width // STEP,),
            in_specs=[
                pl.BlockSpec((z_size, z_size, LISTS), lambda i, order: (0, tok_count // z_size, 0)),
                pl.BlockSpec((z_size, tok_count, STEP), lambda i, order: (0, 0, i)),
                pl.BlockSpec(after.shape, lambda i, order: (0, 0)),
            ],
            out_specs=pl.BlockSpec((plane, count, capacity, STEP), lambda i, order: (0, 0, 0, i)),
        ),
        out_shape=jax.ShapeDtypeStruct((plane, count, capacity, width), jnp.bfloat16),
        name="pack_far",
    )(order, blocks, blocks, after)


def mix_far_kernel(order_ref, lists_ref, rows_ref, out_ref):
    plane, count, capacity, width = rows_ref.shape
    for i in range(len(NEAR)):
        out_ref[order_ref[i]] = jnp.zeros(out_ref.shape[1:], out_ref.dtype)
    for i in range(count):
        src = order_ref[len(NEAR) + i]
        lists = lists_of(lists_ref[src], order_ref[0], plane * capacity)
        rows = rows_ref[:, i].reshape(plane * capacity, width)
        out_ref[src] = mixed(lists, rows, out_ref.shape[1]).astype(out_ref.dtype)


def mix_far(order, blocks, rows, tok_count):
    plane, count, capacity, width = rows.shape
    z_size = blocks.shape[0]
    return pl.pallas_call(
        mix_far_kernel,
        grid_spec=pltpu.PrefetchScalarGridSpec(
            num_scalar_prefetch=1,
            grid=(width // STEP,),
            in_specs=[
                pl.BlockSpec((z_size, z_size, LISTS), lambda i, order: (0, tok_count // z_size, 0)),
                pl.BlockSpec((plane, count, capacity, STEP), lambda i, order: (0, 0, 0, i)),
            ],
            out_specs=pl.BlockSpec((z_size, tok_count, STEP), lambda i, order: (0, 0, i)),
        ),
        out_shape=jax.ShapeDtypeStruct((z_size, tok_count, width), jnp.bfloat16),
        name="mix_far",
    )(order, blocks, rows)


def mix_near_kernel(order_ref, *refs):
    count = len(NEAR)
    rows_ref, outs = refs[count], refs[count + 1 :]
    plane, _, capacity, width = rows_ref.shape
    for i in range(count):
        lists = lists_of(refs[i][...], order_ref[0], plane * capacity)
        rows = rows_ref[:, i].reshape(plane * capacity, width)
        outs[i][...] = mixed(lists, rows, outs[i].shape[0]).astype(outs[i].dtype)


def mix_near(order, blocks, rows, tok_count):
    plane, count, capacity, width = rows.shape
    z_size = blocks[0].shape[0] - tok_count
    kinds = [jnp.bfloat16 if offset else jnp.float32 for offset in NEAR]
    return pl.pallas_call(
        mix_near_kernel,
        grid_spec=pltpu.PrefetchScalarGridSpec(
            num_scalar_prefetch=1,
            grid=(width // STEP,),
            in_specs=[pl.BlockSpec((z_size, LISTS), lambda i, order: (tok_count // z_size, 0))]
            * count
            + [pl.BlockSpec((plane, count, capacity, STEP), lambda i, order: (0, 0, 0, i))],
            out_specs=[pl.BlockSpec((tok_count, STEP), lambda i, order: (0, i))] * count,
        ),
        out_shape=[jax.ShapeDtypeStruct((tok_count, width), kind) for kind in kinds],
        name="mix_near",
    )(order, *blocks, rows)


def hidden_kernel(near_ref, far_ref, *refs):
    *weights, out_near, out_far, gate_acc, up_acc = refs
    step, steps = pl.program_id(0), pl.num_programs(0)
    gate, gate_other, up, up_other = (ref[...] for ref in weights)
    gate = jnp.concatenate([gate, gate_other], axis=1)
    up = jnp.concatenate([up, up_other], axis=1)
    rows = jnp.concatenate([near_ref[...], far_ref[...]], axis=0)

    @pl.when(step == 0)
    def _():
        gate_acc[...] = dot(rows, gate)
        up_acc[...] = dot(rows, up)

    @pl.when((step > 0) & (step < steps - 1))
    def _():
        gate_acc[...] += dot(rows, gate)
        up_acc[...] += dot(rows, up)

    @pl.when(step == steps - 1)
    def _():
        hidden = jax.nn.silu(gate_acc[...] + dot(rows, gate)) * (up_acc[...] + dot(rows, up))
        count = out_near.shape[0]
        out_near[...] = hidden[:count].astype(out_near.dtype)
        out_far[...] = hidden[count:].astype(out_far.dtype)


def hidden_of(near, far, weights):
    depth, units = weights[0].shape
    counts = [near.shape[0], far.shape[0]]
    return pl.pallas_call(
        hidden_kernel,
        grid=(depth // DEPTH,),
        in_specs=[pl.BlockSpec((c, DEPTH), lambda i: (0, i)) for c in counts]
        + [pl.BlockSpec((DEPTH, units), lambda i: (i, 0))] * 4,
        out_specs=[pl.BlockSpec((c, 2 * units), lambda i: (0, 0)) for c in counts],
        out_shape=[jax.ShapeDtypeStruct((c, 2 * units), jnp.bfloat16) for c in counts],
        scratch_shapes=[pltpu.VMEM((sum(counts), 2 * units), jnp.float32)] * 2,
        compiler_params=pltpu.CompilerParams(vmem_limit_bytes=56 << 20),
        name="hidden",
    )(near, far, *weights)


def dot(a, b):
    return jnp.dot(a, b, preferred_element_type=jnp.float32)


def body(tokens, routes, gate_probs, gate_w, up_w, down_w):
    sizes = tuple(lax.axis_size(a) for a in ("x", "z", "y"))
    x_size, z_size, y_size = sizes
    plane = x_size * y_size
    tok_count, model_width = tokens.shape
    capacity = 2 * tok_count * routes.shape[1] // (plane * z_size)
    my_z = lax.axis_index("z")
    up_ring = [(i, (i + 1) % z_size) for i in range(z_size)]
    down_ring = [(i, (i - 1) % z_size) for i in range(z_size)]

    def in_plane(rows, count):
        rows = rows.reshape(plane, count * capacity, model_width)
        rows = lax.all_to_all(rows, ("x", "y"), split_axis=0, concat_axis=0, tiled=True)
        return rows.reshape(plane, count, capacity, model_width)

    def flat(rows):
        return rows.reshape(-1, model_width)

    offsets = [*NEAR, *(d for d in range(2, z_size - 1))]
    near_count, far_count = len(NEAR), z_size - len(NEAR)
    order = jnp.stack([my_z + d for d in offsets]) % z_size

    table = slot_table(routes, gate_probs, sizes, capacity).reshape(z_size, -1)
    table = jnp.pad(table, ((0, 0), (0, model_width - table.shape[1])))
    block = jnp.concatenate([tokens, table], axis=0)
    blocks = lax.all_gather(block, "z", axis=0, tiled=False)
    near_blocks = [block, lax.ppermute(block, "z", up_ring), lax.ppermute(block, "z", down_ring)]

    swap = [(0, 1), (1, 0)]
    weights = [gate_w[0], up_w[0]]
    weights = [v for w in weights for v in (w, lax.ppermute(w, "dp", swap))]
    w_down = jnp.concatenate([down_w[0], lax.ppermute(down_w[0], "dp", swap)], axis=0)

    weights, w_down, near_blocks, order = lax.optimization_barrier(
        (weights, w_down, near_blocks, order)
    )
    near = flat(in_plane(pack_near(order, near_blocks, tok_count, plane, capacity), near_count))
    after = near[:8, :128] + 1
    far = pack_far(order, blocks, after, tok_count, plane, capacity)
    far = flat(in_plane(far, far_count))
    hidden_near, hidden_far = hidden_of(near, far, weights)

    answers = dot(hidden_far, w_down).astype(jnp.bfloat16)
    answers = in_plane(answers, far_count)
    partial = mix_far(order, blocks, answers, tok_count)
    partial, hidden_near = lax.optimization_barrier((partial, hidden_near))
    total = lax.psum_scatter(partial, "z", scatter_dimension=0, tiled=True)[0]

    answers = dot(hidden_near, w_down).astype(jnp.bfloat16)
    answers = in_plane(answers, near_count)
    own, under, over = mix_near(order, near_blocks, answers, tok_count)
    under, over = lax.ppermute(under, "z", down_ring), lax.ppermute(over, "z", up_ring)
    total = total.astype(jnp.float32) + own + under.astype(jnp.float32) + over.astype(jnp.float32)
    return total.astype(jnp.bfloat16)


def solution(mesh):
    experts, dp = mesh.shape["expert"], mesh.shape["dp"]
    x_size = y_size = 4
    z_size = experts // (x_size * y_size)
    grid = Mesh(mesh.devices.reshape(x_size, z_size, y_size, dp), ("x", "z", "y", "dp"))
    every, owner = ("x", "z", "y", "dp"), ("x", "z", "y")
    return jax.shard_map(
        body,
        mesh=grid,
        in_specs=(
            P(every, None),
            P(every, None),
            P(every, None),
            P(owner, None, "dp"),
            P(owner, None, "dp"),
            P(owner, "dp", None),
        ),
        out_specs=P(every, None),
        check_vma=False,
    )
```

```python
import functools

import jax
import jax.numpy as jnp
import numpy as np
from jax import lax
from jax.experimental import pallas as pl
from jax.experimental.pallas import tpu as pltpu
from jax.sharding import Mesh
from jax.sharding import PartitionSpec as P

DEPTH = 512
STEP = 2048
LISTS = 512
NEAR = (0, -1, 1)


def slot_table(routes, gate_probs, sizes, capacity):
    x_size, z_size, y_size = sizes
    tok_count, top_count = routes.shape
    flat = routes.T.reshape(-1)
    token = jnp.arange(tok_count * top_count, dtype=jnp.int32) % tok_count
    earlier = (flat[:, None] == flat[None, :]) & (token[None, :] < token[:, None])
    slot = jnp.sum(earlier.astype(jnp.int32), axis=1)
    ex, ez, ey = flat // (z_size * y_size), flat // y_size % z_size, flat % y_size
    target = ((ez * x_size + ex) * y_size + ey) * capacity + slot
    slots = jnp.arange(x_size * z_size * y_size * capacity, dtype=jnp.int32)
    here = target[None, :] == slots[:, None]
    held = jnp.sum(jnp.where(here, (token + 1).astype(jnp.float32)[None, :], 0.0), axis=1)
    prob = jnp.sum(jnp.where(here, gate_probs.T.reshape(-1)[None, :], 0.0), axis=1)
    high = lax.reduce_precision(prob, 8, 7)
    table = jnp.stack([held, high, prob - high]).reshape(3, z_size, -1)
    return table.transpose(1, 0, 2).astype(jnp.bfloat16)


def hits(row_token, tok_count):
    tokens = lax.broadcasted_iota(jnp.int32, (tok_count, row_token.shape[1]), 0)
    return tokens == row_token.astype(jnp.int32) - 1


def place_rows(here, block):
    place = jnp.where(here, 1.0, 0.0).astype(jnp.bfloat16)
    rows = lax.dot_general(
        place, block, (((0,), (0,)), ((), ())), preferred_element_type=jnp.float32
    )
    return rows.astype(jnp.bfloat16)


def lists_of(rows, me, lanes):
    rows = rows[:, : 3 * lanes].astype(jnp.float32)
    mine = lax.broadcasted_iota(jnp.int32, rows.shape, 0) == me
    rows = jnp.sum(jnp.where(mine, rows, 0.0), axis=0, keepdims=True)
    return [rows[:, r * lanes : (r + 1) * lanes] for r in range(3)]


def kept_lists(kept, i, rows_ref, me, lanes):
    @pl.when(pl.program_id(0) == 0)
    def _():
        for r, part in enumerate(lists_of(rows_ref[...], me, lanes)):
            kept[i, r : r + 1, :] = part

    return [kept[i, r : r + 1, :] for r in range(3)]


def mixed(lists, rows, tok_count):
    here = hits(lists[0], tok_count)
    both = jnp.concatenate([jnp.where(here, part, 0.0) for part in lists[1:]], axis=0)
    sums = jnp.dot(both.astype(jnp.bfloat16), rows, preferred_element_type=jnp.float32)
    return sums[:tok_count] + sums[tok_count:]


def pack_near_kernel(order_ref, *refs):
    *list_refs, out_ref, kept = refs
    count = len(list_refs) // 2
    plane, _, capacity, width = out_ref.shape
    for i in range(count):
        token_ref = list_refs[count + i]
        lists = kept_lists(kept, i, list_refs[i], order_ref[0], plane * capacity)
        rows = place_rows(hits(lists[0], token_ref.shape[0]), token_ref[...])
        out_ref[:, i] = rows.reshape(plane, capacity, width)


def pack_near(order, blocks, tok_count, plane, capacity):
    count, width = len(blocks), blocks[0].shape[1]
    z_size = blocks[0].shape[0] - tok_count
    below = pl.BlockSpec((z_size, LISTS), lambda i, order: (tok_count // z_size, 0))
    return pl.pallas_call(
        pack_near_kernel,
        grid_spec=pltpu.PrefetchScalarGridSpec(
            num_scalar_prefetch=1,
            grid=(width // STEP,),
            in_specs=[below] * count
            + [pl.BlockSpec((tok_count, STEP), lambda i, order: (0, i))] * count,
            out_specs=pl.BlockSpec((plane, count, capacity, STEP), lambda i, order: (0, 0, 0, i)),
            scratch_shapes=[pltpu.VMEM((count, 3, plane * capacity), jnp.float32)],
        ),
        out_shape=jax.ShapeDtypeStruct((plane, count, capacity, width), jnp.bfloat16),
        name="pack_near",
    )(order, *blocks, *blocks)


def pack_far_kernel(order_ref, lists_ref, tok_ref, _, out_ref, kept):
    plane, count, capacity, width = out_ref.shape
    for i in range(count):
        src = order_ref[len(NEAR) + i]
        lists = kept_lists(kept, i, lists_ref.at[src], order_ref[0], plane * capacity)
        rows = place_rows(hits(lists[0], tok_ref.shape[1]), tok_ref[src])
        out_ref[:, i] = rows.reshape(plane, capacity, width)


def pack_far(order, blocks, after, tok_count, plane, capacity):
    z_size, _, width = blocks.shape
    count = z_size - len(NEAR)
    return pl.pallas_call(
        pack_far_kernel,
        grid_spec=pltpu.PrefetchScalarGridSpec(
            num_scalar_prefetch=1,
            grid=(width // STEP,),
            in_specs=[
                pl.BlockSpec((z_size, z_size, LISTS), lambda i, order: (0, tok_count // z_size, 0)),
                pl.BlockSpec((z_size, tok_count, STEP), lambda i, order: (0, 0, i)),
                pl.BlockSpec(after.shape, lambda i, order: (0, 0)),
            ],
            out_specs=pl.BlockSpec((plane, count, capacity, STEP), lambda i, order: (0, 0, 0, i)),
            scratch_shapes=[pltpu.VMEM((count, 3, plane * capacity), jnp.float32)],
        ),
        out_shape=jax.ShapeDtypeStruct((plane, count, capacity, width), jnp.bfloat16),
        name="pack_far",
    )(order, blocks, blocks, after)


def mix_far_kernel(order_ref, lists_ref, rows_ref, out_ref, kept):
    plane, count, capacity, width = rows_ref.shape
    for i in range(len(NEAR)):
        out_ref[order_ref[i]] = jnp.zeros(out_ref.shape[1:], out_ref.dtype)
    for i in range(count):
        src = order_ref[len(NEAR) + i]
        lists = kept_lists(kept, i, lists_ref.at[src], order_ref[0], plane * capacity)
        rows = rows_ref[:, i].reshape(plane * capacity, width)
        out_ref[src] = mixed(lists, rows, out_ref.shape[1]).astype(out_ref.dtype)


def mix_far(order, blocks, rows, tok_count):
    plane, count, capacity, width = rows.shape
    z_size = blocks.shape[0]
    return pl.pallas_call(
        mix_far_kernel,
        grid_spec=pltpu.PrefetchScalarGridSpec(
            num_scalar_prefetch=1,
            grid=(width // STEP,),
            in_specs=[
                pl.BlockSpec((z_size, z_size, LISTS), lambda i, order: (0, tok_count // z_size, 0)),
                pl.BlockSpec((plane, count, capacity, STEP), lambda i, order: (0, 0, 0, i)),
            ],
            out_specs=pl.BlockSpec((z_size, tok_count, STEP), lambda i, order: (0, 0, i)),
            scratch_shapes=[pltpu.VMEM((count, 3, plane * capacity), jnp.float32)],
        ),
        out_shape=jax.ShapeDtypeStruct((z_size, tok_count, width), jnp.bfloat16),
        name="mix_far",
    )(order, blocks, rows)


def mix_near_kernel(order_ref, *refs):
    count = len(NEAR)
    rows_ref, *outs, kept = refs[count:]
    plane, _, capacity, width = rows_ref.shape
    for i in range(count):
        lists = kept_lists(kept, i, refs[i], order_ref[0], plane * capacity)
        rows = rows_ref[:, i].reshape(plane * capacity, width)
        outs[i][...] = mixed(lists, rows, outs[i].shape[0]).astype(outs[i].dtype)


def mix_near(order, blocks, rows, tok_count):
    plane, count, capacity, width = rows.shape
    z_size = blocks[0].shape[0] - tok_count
    kinds = [jnp.bfloat16 if offset else jnp.float32 for offset in NEAR]
    return pl.pallas_call(
        mix_near_kernel,
        grid_spec=pltpu.PrefetchScalarGridSpec(
            num_scalar_prefetch=1,
            grid=(width // STEP,),
            in_specs=[pl.BlockSpec((z_size, LISTS), lambda i, order: (tok_count // z_size, 0))]
            * count
            + [pl.BlockSpec((plane, count, capacity, STEP), lambda i, order: (0, 0, 0, i))],
            out_specs=[pl.BlockSpec((tok_count, STEP), lambda i, order: (0, i))] * count,
            scratch_shapes=[pltpu.VMEM((count, 3, plane * capacity), jnp.float32)],
        ),
        out_shape=[jax.ShapeDtypeStruct((tok_count, width), kind) for kind in kinds],
        name="mix_near",
    )(order, *blocks, rows)


def hidden_kernel(near_ref, far_ref, *refs):
    *weights, out_near, out_far, gate_acc, up_acc = refs
    step, steps = pl.program_id(0), pl.num_programs(0)
    gate, gate_other, up, up_other = (ref[...] for ref in weights)
    gate = jnp.concatenate([gate, gate_other], axis=1)
    up = jnp.concatenate([up, up_other], axis=1)
    rows = jnp.concatenate([near_ref[...], far_ref[...]], axis=0)

    @pl.when(step == 0)
    def _():
        gate_acc[...] = dot(rows, gate)
        up_acc[...] = dot(rows, up)

    @pl.when((step > 0) & (step < steps - 1))
    def _():
        gate_acc[...] += dot(rows, gate)
        up_acc[...] += dot(rows, up)

    @pl.when(step == steps - 1)
    def _():
        hidden = jax.nn.silu(gate_acc[...] + dot(rows, gate)) * (up_acc[...] + dot(rows, up))
        count = out_near.shape[0]
        out_near[...] = hidden[:count].astype(out_near.dtype)
        out_far[...] = hidden[count:].astype(out_far.dtype)


def hidden_of(near, far, weights):
    depth, units = weights[0].shape
    counts = [near.shape[0], far.shape[0]]
    return pl.pallas_call(
        hidden_kernel,
        grid=(depth // DEPTH,),
        in_specs=[pl.BlockSpec((c, DEPTH), lambda i: (0, i)) for c in counts]
        + [pl.BlockSpec((DEPTH, units), lambda i: (i, 0))] * 4,
        out_specs=[pl.BlockSpec((c, 2 * units), lambda i: (0, 0)) for c in counts],
        out_shape=[jax.ShapeDtypeStruct((c, 2 * units), jnp.bfloat16) for c in counts],
        scratch_shapes=[pltpu.VMEM((sum(counts), 2 * units), jnp.float32)] * 2,
        compiler_params=pltpu.CompilerParams(vmem_limit_bytes=56 << 20),
        name="hidden",
    )(near, far, *weights)


def dot(a, b):
    return jnp.dot(a, b, preferred_element_type=jnp.float32)


def body(tokens, routes, gate_probs, gate_w, up_w, down_w):
    sizes = tuple(lax.axis_size(a) for a in ("x", "z", "y"))
    x_size, z_size, y_size = sizes
    plane = x_size * y_size
    tok_count, model_width = tokens.shape
    capacity = 2 * tok_count * routes.shape[1] // (plane * z_size)
    my_z = lax.axis_index("z")
    up_ring = [(i, (i + 1) % z_size) for i in range(z_size)]
    down_ring = [(i, (i - 1) % z_size) for i in range(z_size)]

    def in_plane(rows, count):
        rows = rows.reshape(plane, count * capacity, model_width)
        rows = lax.all_to_all(rows, ("x", "y"), split_axis=0, concat_axis=0, tiled=True)
        return rows.reshape(plane, count, capacity, model_width)

    def flat(rows):
        return rows.reshape(-1, model_width)

    offsets = [*NEAR, *(d for d in range(2, z_size - 1))]
    near_count, far_count = len(NEAR), z_size - len(NEAR)
    order = jnp.stack([my_z + d for d in offsets]) % z_size

    table = slot_table(routes, gate_probs, sizes, capacity).reshape(z_size, -1)
    table = jnp.pad(table, ((0, 0), (0, model_width - table.shape[1])))
    block = jnp.concatenate([tokens, table], axis=0)
    blocks = lax.all_gather(block, "z", axis=0, tiled=False)
    near_blocks = [block, lax.ppermute(block, "z", up_ring), lax.ppermute(block, "z", down_ring)]

    swap = [(0, 1), (1, 0)]
    weights = [gate_w[0], up_w[0]]
    weights = [v for w in weights for v in (w, lax.ppermute(w, "dp", swap))]
    w_down = jnp.concatenate([down_w[0], lax.ppermute(down_w[0], "dp", swap)], axis=0)

    weights, w_down, near_blocks, order = lax.optimization_barrier(
        (weights, w_down, near_blocks, order)
    )
    near = flat(in_plane(pack_near(order, near_blocks, tok_count, plane, capacity), near_count))
    after = near[:8, :128] + 1
    far = pack_far(order, blocks, after, tok_count, plane, capacity)
    far = flat(in_plane(far, far_count))
    hidden_near, hidden_far = hidden_of(near, far, weights)

    answers = dot(hidden_far, w_down).astype(jnp.bfloat16)
    answers = in_plane(answers, far_count)
    partial = mix_far(order, blocks, answers, tok_count)
    partial, hidden_near = lax.optimization_barrier((partial, hidden_near))
    total = lax.psum_scatter(partial, "z", scatter_dimension=0, tiled=True)[0]

    answers = dot(hidden_near, w_down).astype(jnp.bfloat16)
    answers = in_plane(answers, near_count)
    own, under, over = mix_near(order, near_blocks, answers, tok_count)
    under, over = lax.ppermute(under, "z", down_ring), lax.ppermute(over, "z", up_ring)
    total = total.astype(jnp.float32) + own + under.astype(jnp.float32) + over.astype(jnp.float32)
    return total.astype(jnp.bfloat16)


def solution(mesh):
    experts, dp = mesh.shape["expert"], mesh.shape["dp"]
    x_size = y_size = 4
    z_size = experts // (x_size * y_size)
    grid = Mesh(mesh.devices.reshape(x_size, z_size, y_size, dp), ("x", "z", "y", "dp"))
    every, owner = ("x", "z", "y", "dp"), ("x", "z", "y")
    return jax.shard_map(
        body,
        mesh=grid,
        in_specs=(
            P(every, None),
            P(every, None),
            P(every, None),
            P(owner, None, "dp"),
            P(owner, None, "dp"),
            P(owner, "dp", None),
        ),
        out_specs=P(every, None),
        check_vma=False,
    )
```
